1024 devices in a mesh: dp: 64 (over z, x), fsdp: 16 (over y, core).
Axes of the slice: x: 4, y: 8, z: 16, core: 2. Of those that a mesh axis runs over, the one named last changes fastest.
Arguments:
- text_states: bfloat16 [192, 64, 4096], P('dp', None, 'fsdp'), may hold values from -6 to 6
- cotangent: bfloat16 [192, 64, 4096], P('dp', None, 'fsdp'), may hold values from -16 to 16
- norm_gain: float32 [4096], replicated, may hold values from 0.5 to 120
- norm_bias: float32 [4096], replicated, may hold values from -3 to 3
- branch_gate: float32 [1], replicated, may hold values from 0.4 to 1.2
- query_weight: bfloat16 [4096, 16, 128], P(None, 'fsdp'), may hold values from -0.09375 to 0.09375
- latent_weight: bfloat16 [4096, 16, 256], P(None, 'fsdp'), may hold values from -0.09375 to 0.09375
- output_weight: bfloat16 [16, 128, 4096], P('fsdp'), may hold values from -0.125 to 0.125
- latents: bfloat16 [576, 64, 4096], P('dp'), may hold values from -6 to 6
- media_refs: int32 [192, 5], replicated, may hold values from -1 to 575, as said below
- media_pos: int32 [192, 64], P('dp'), may hold values from -1 to 4, as said below
- owner_map: int32 [576], replicated, may hold values from 0 to 575, as said below
Outputs:
- layer_out: bfloat16 [192, 64, 4096], P('dp', None, 'fsdp')
- out_grad: float32 [16, 128, 4096], P('fsdp', None, 'dp')
The draws below stay inside these ranges and needn't reach their ends.
Inputs may be any that keep to these rules, and one draw needn't show every extreme that they name: `media_refs`: row s holds the ids of sequence s's images in its first 1 to 5 entries, the rest are -1; every image id stands in exactly one row. A permutation: image i's latents are storage row owner_map[i], held by data shard owner_map[i] // 9. The images of one data shard's sequences lie on at most 1 storage rows of any one data shard, and some data shard reaches 1. `media_pos`: for each token, the number of its sequence's images placed at or before it, minus one; images take increasing positions in the window, each image has tokens, and a slot named is always filled in media_refs.
All inputs are finite; a program needn't handle non-finite values.
Results may differ from the reference program's by a relative error of at most 0.039.
The reference program's roundings to bfloat16 on the way count: a program that leaves them out, or rounds other values in their place, can miss the bound.
Values may be sent and summed in bfloat16 or wider, within the bound.
A program may use at most 64 MiB of HBM per device.

```python
import jax
import jax.numpy as jnp
from jax import lax

D = 4096
HEADS = 16
HD = 128
LAT = 64
MAXIMG = 5
SEQ_DP = 3
WIN = 64
SEQS = 192
IMG_DP = 9
IMAGES = 576


def media_plan(key):
    count_key = jax.random.fold_in(key, 101)
    order_key = jax.random.fold_in(key, 102)
    owner_key = jax.random.fold_in(key, 103)
    shift_key = jax.random.fold_in(key, 104)
    turn_key = jax.random.fold_in(key, 105)
    place_key = jax.random.fold_in(key, 106)
    start_key = jax.random.fold_in(key, 107)
    groups = SEQS // SEQ_DP
    half_count = SEQS // 2
    first_half = jax.random.randint(count_key, (half_count,), 1, MAXIMG + 1)
    first_half = jnp.where(jnp.arange(half_count) < SEQ_DP, MAXIMG, first_half)
    counts = jnp.concatenate([first_half, MAXIMG + 1 - first_half]).astype(jnp.int32)
    offsets = jnp.cumsum(counts) - counts
    entry = jnp.arange(MAXIMG, dtype=jnp.int32)
    order_slot = offsets[:, None] + entry[None, :]
    live = entry[None, :] < counts[:, None]
    image_order = jax.random.permutation(order_key, IMAGES).astype(jnp.int32)
    refs = jnp.where(live, image_order[jnp.minimum(order_slot, IMAGES - 1)], -1).astype(jnp.int32)
    owner_order = jax.random.permutation(owner_key, groups).astype(jnp.int32)
    shift_amount = jax.random.randint(shift_key, (), 0, groups)
    turns = jax.random.randint(turn_key, (groups,), 0, IMG_DP)
    ranked = jnp.arange(IMAGES, dtype=jnp.int32) + shift_amount
    residue = ranked % groups
    within = (ranked // groups + turns[residue]) % IMG_DP
    storage = owner_order[residue] * IMG_DP + within
    owners = jnp.zeros((IMAGES,), jnp.int32).at[image_order].set(storage.astype(jnp.int32))
    first_place = jax.random.randint(start_key, (SEQS, 1), 0, max(WIN // 8, 1))
    gaps = jax.random.randint(place_key, (SEQS, MAXIMG - 1), 1, max(WIN // MAXIMG, 2))
    places = jnp.concatenate([first_place, first_place + jnp.cumsum(gaps, axis=1)], axis=1)
    token_index = jnp.arange(WIN, dtype=jnp.int32)
    seen = (places[:, None, :] <= token_index[None, :, None]) & live[:, None, :]
    positions = (jnp.sum(seen.astype(jnp.int32), axis=-1) - 1).astype(jnp.int32)
    return (refs, owners, positions)


def draw_media_refs(key, part):
    return media_plan(key)[0]


def draw_owner_map(key, part):
    return media_plan(key)[1]


def draw_media_pos(key, part):
    return media_plan(key)[2]


def draw_norm_gain(key, part):
    spread = jax.random.truncated_normal(jax.random.fold_in(key, 302), -5.0, 5.0, (D,), jnp.float32)
    return (1.0 + 0.1 * spread).astype(jnp.float32)


def raised(drawn, key, source, target, blocks, factor):
    def block_of(dim):
        return (jnp.arange(drawn.shape[dim]) // (drawn.shape[dim] // blocks)).reshape((-1,) + (1,) * (drawn.ndim - 1 - dim))

    near = jax.random.permutation(key, blocks)[block_of(target)]
    far = (block_of(target) + blocks // 2) % blocks
    return jnp.where((block_of(source) == near) | (block_of(source) == far), factor * drawn, drawn)


def shard_levels(own_key, extent, split, smallest, high):
    factor_of, own = 1.0, jax.random.fold_in(own_key, 6)
    for axis_at, blocks in split:
        draws = jnp.exp(jax.random.uniform(jax.random.fold_in(own, axis_at), (blocks,), jnp.float32, smallest / len(split), high / len(split)))
        factor_of = factor_of * jnp.repeat(draws, extent[axis_at] // blocks).reshape([-1 if axis == axis_at else 1 for axis in range(len(extent))])
    return factor_of


def scatter_about(own_key, shape, scale, reach, pieces=(), held_as=jnp.bfloat16):
    level = shard_levels(own_key, shape, pieces, -0.22, 0.18) if pieces else 1.0
    array = jax.random.normal(own_key, shape, jnp.float32) * scale * level
    return jnp.minimum(jnp.maximum(array, -reach), reach).astype(held_as)


def heavy_noise(key, extent, scale, most, shards, heavy, held_as=jnp.bfloat16):
    drawn = scale * jax.random.normal(key, extent, jnp.float32)
    if shards:
        drawn = drawn * shard_levels(key, extent, shards, -0.22, 0.18)
    return jnp.clip(raised(drawn, jax.random.fold_in(key, 3), *heavy), -most, most).astype(held_as)


def setup_inputs(seed: int = 0) -> dict:
    streams_of = jax.random.split(jax.random.key(seed), 13)
    text_states = scatter_about(streams_of[0], (SEQS, WIN, D), 1.0, 6.0, ((0, 64), (2, 16)))
    cotangent = heavy_noise(streams_of[1], (SEQS, WIN, D), 1.0, 16.0, ((0, 64), (2, 16)), (0, 2, 64, 4.0))
    norm_gain = draw_norm_gain(jax.random.fold_in(streams_of[12], 71), 0)
    norm_bias = scatter_about(streams_of[3], (D,), 0.5, 3.0, (), jnp.float32)
    branch_gate = jnp.clip(jax.random.uniform(streams_of[4], (1,), jnp.float32, 0.4, 1.2), 0.4, 1.2)
    query_weight = scatter_about(streams_of[5], (D, HEADS, HD), D ** -0.5, 0.09375, ((1, 16),))
    latent_weight = scatter_about(streams_of[6], (D, HEADS, 2 * HD), D ** -0.5, 0.09375, ((1, 16),))
    output_weight = scatter_about(streams_of[7], (HEADS, HD, D), (HEADS * HD) ** -0.5, 0.125, ((0, 16),))
    latents = scatter_about(streams_of[8], (IMAGES, LAT, D), 1.0, 6.0, ((0, 64),))
    media_refs = draw_media_refs(jax.random.fold_in(streams_of[12], 71), 0)
    media_pos = draw_media_pos(jax.random.fold_in(streams_of[12], 71), 0)
    owner_map = draw_owner_map(jax.random.fold_in(streams_of[12], 71), 0)
    return {"text_states": text_states, "cotangent": cotangent, "norm_gain": norm_gain, "norm_bias": norm_bias, "branch_gate": branch_gate, "query_weight": query_weight, "latent_weight": latent_weight, "output_weight": output_weight, "latents": latents, "media_refs": media_refs, "media_pos": media_pos, "owner_map": owner_map}


def reference(text_states, cotangent, norm_gain, norm_bias, branch_gate, query_weight, latent_weight, output_weight, latents, media_refs, media_pos, owner_map):
    tokens = SEQS * WIN
    as_float = text_states.astype(jnp.float32).reshape(tokens, D)
    row_mean = lax.optimization_barrier(jnp.mean(as_float, axis=-1, keepdims=True))
    centered = as_float - row_mean
    variance = lax.optimization_barrier(jnp.mean(centered * centered, axis=-1, keepdims=True))
    normed = (centered * lax.rsqrt(variance + 1e-05) * norm_gain + norm_bias).astype(jnp.bfloat16)
    queries = jnp.dot(normed, query_weight.reshape(D, HEADS * HD), preferred_element_type=jnp.float32)
    queries = (queries * HD ** (-0.5)).astype(jnp.bfloat16).reshape(SEQS, WIN, HEADS, HD)
    pairs = jnp.dot(latents.reshape(IMAGES * LAT, D), latent_weight.reshape(D, HEADS * 2 * HD), preferred_element_type=jnp.float32)
    pairs = pairs.astype(jnp.bfloat16).reshape(IMAGES, LAT, HEADS, 2 * HD)
    ref_storage = owner_map[jnp.maximum(media_refs, 0)].astype(jnp.int32)
    column_image = jnp.arange(MAXIMG * LAT, dtype=jnp.int32) // LAT

    def one_sequence(packed):
        query_block, position, storage = packed
        block = pairs[storage].reshape(MAXIMG * LAT, HEADS, 2 * HD)
        key_part = block[:, :, :HD].astype(jnp.float32)
        value_part = block[:, :, HD:].astype(jnp.float32)
        scores = jnp.einsum('the,mhe->htm', query_block.astype(jnp.float32), key_part)
        allowed = position[:, None] == column_image[None, :]
        scores = jnp.where(allowed[None], scores, -1e+30)
        row_max = lax.optimization_barrier(jnp.max(scores, axis=-1, keepdims=True))
        weights = jnp.exp(scores - row_max)
        softmaxed = (weights / lax.optimization_barrier(jnp.sum(weights, axis=-1, keepdims=True))).astype(jnp.bfloat16)
        context = jnp.einsum('htm,mhe->the', softmaxed.astype(jnp.float32), value_part)
        context = jnp.where(position[:, None, None] >= 0, context, 0.0)
        return context.astype(jnp.bfloat16)
    context = lax.map(one_sequence, (queries, media_pos, ref_storage))
    context_rows = context.reshape(tokens, HEADS * HD)
    update = jnp.dot(context_rows, output_weight.reshape(HEADS * HD, D), preferred_element_type=jnp.float32)
    gate_scale = jnp.tanh(branch_gate[0])
    layer_out = (as_float + gate_scale * update).reshape(SEQS, WIN, D).astype(jnp.bfloat16)
    gradient = jnp.dot(context_rows.T, cotangent.reshape(tokens, D), preferred_element_type=jnp.float32)
    out_grad = (gate_scale * gradient).reshape(HEADS, HD, D)
    return (layer_out, out_grad)
```

```python
import functools

import jax
import jax.numpy as jnp
from jax import lax
from jax.experimental import pallas as pl
from jax.experimental.pallas import tpu as pltpu
from jax.sharding import Mesh
from jax.sharding import PartitionSpec as P

EPSILON = 1e-05
MESH = pl.DeviceIdType.MESH
NZ, NX, NY = 16, 4, 8
GROUP = 2 * NY
IMG = 9
LAT = 64
TOK = 192
CHUNKS = 3
CHUNK_ROWS = IMG * LAT // CHUNKS
HALF_Z = NZ // 2
HALF_Y = NY // 2
BF16 = jnp.bfloat16
F32 = jnp.float32


def remote(src, dst, send, recv, where):
    return pltpu.make_async_remote_copy(
        src_ref=src, dst_ref=dst, send_sem=send, recv_sem=recv, device_id=where, device_id_type=MESH
    )


def position():
    return lax.axis_index("z"), lax.axis_index("x"), lax.axis_index("y"), lax.axis_index("c")


def meet(targets):
    barrier = pltpu.get_barrier_semaphore()
    for where in targets:
        pl.semaphore_signal(barrier, inc=1, device_id=where, device_id_type=MESH)
    return lambda: pl.semaphore_wait(barrier, len(targets))


def fsdp_peers(y, c):
    peers = [{"c": 1 - c}]
    for dy in range(1, NY):
        for dc in range(2):
            peers.append({"y": lax.rem(y + dy, NY), "c": lax.rem(c + dc, 2)})
    return peers


def x_peers(x):
    return [{"x": lax.rem(x + dx, NX)} for dx in range(1, NX)]


class YRing:
    def __init__(self, own, full, y, c, send, recv, psend, precv):
        self.own, self.full, self.y, self.c = own, full, y, c
        self.send, self.recv, self.psend, self.precv = send, recv, psend, precv
        self.started = []

    def slot(self, direction, k, core):
        row = lax.rem(self.y + (NY - k if direction == 0 else k), NY)
        return self.full.at[2 * row + core]

    def neighbour(self, direction):
        return {"y": lax.rem(self.y + (1 if direction == 0 else NY - 1), NY)}

    def hop(self, direction, k):
        src = self.own if k == 1 else self.slot(direction, k - 1, self.c)
        dst = self.slot(direction, k - 1, self.c)
        copy = remote(src, dst, self.send.at[direction, k], self.recv.at[direction, k], self.neighbour(direction))
        copy.start()
        self.started.append(copy)

    def to_partner(self, src, dst, index):
        copy = remote(src, dst, self.psend.at[index], self.precv.at[index], {"c": 1 - self.c})
        copy.start()
        self.started.append(copy)

    def begin(self):
        self.hop(0, 1)
        self.hop(1, 1)
        mine = self.slot(0, 0, self.c)
        self.to_partner(self.own, mine, 0)
        pltpu.sync_copy(self.own, mine)

    def step(self, k):
        for direction, last in ((0, HALF_Y), (1, HALF_Y - 1)):
            if k <= last:
                here = self.slot(direction, k, self.c)
                remote(
                    here, here, self.send.at[direction, k], self.recv.at[direction, k], self.neighbour(direction)
                ).wait_recv()
                if k < last:
                    self.hop(direction, k + 1)
                self.to_partner(here, here, k + (HALF_Y if direction else 0))

    def finish(self):
        for direction, last in ((0, HALF_Y), (1, HALF_Y - 1)):
            for k in range(0 if direction == 0 else 1, last + 1):
                index = k + (HALF_Y if direction else 0)
                there = self.slot(direction, k, 1 - self.c)
                remote(
                    there, there, self.psend.at[index], self.precv.at[index], {"c": 1 - self.c}
                ).wait_recv()
        for copy in self.started:
            copy.wait_send()


def gather_kernel(
    sel_ref,
    pairs_ref,
    text_ref,
    cot_ref,
    wo_ref,
    kv_ref,
    text_all,
    cot_all,
    wo_all,
    picked,
    zsend,
    zrecv,
    xsend,
    xrecv,
    tsend,
    trecv,
    tpsend,
    tprecv,
    csend,
    crecv,
    cpsend,
    cprecv,
    wsend,
    wrecv,
    *slots,
):
    z, x, y, c = position()
    me = 2 * y + c
    fsdp = fsdp_peers(y, c)
    ups = ({"z": lax.rem(z + 1, NZ)}, {"z": lax.rem(z + NZ - 1, NZ)})
    meet([*ups, *x_peers(x), *fsdp])()

    held = ([pairs_ref, *slots[:HALF_Z]], [pairs_ref, *slots[HALF_Z:]] + [slots[HALF_Z - 1]])

    def exists(direction, k, ch):
        return k < HALF_Z or (k == HALF_Z and (ch == CHUNKS - 1) == (direction == 1))

    def zcopy(direction, k, ch):
        rows = pl.ds(ch * CHUNK_ROWS, CHUNK_ROWS)
        return remote(
            held[direction][k - 1].at[rows],
            held[direction][k].at[rows],
            zsend.at[direction, k, ch],
            zrecv.at[direction, k, ch],
            ups[direction],
        )

    zcopies = {
        (d, k, ch): zcopy(d, k, ch)
        for k in range(1, HALF_Z + 1)
        for ch in range(CHUNKS)
        for d in range(2)
        if exists(d, k, ch)
    }
    for ch in range(CHUNKS):
        for d in range(2):
            zcopies[d, 1, ch].start()

    text_ring = YRing(text_ref, text_all, y, c, tsend, trecv, tpsend, tprecv)
    cot_ring = YRing(cot_ref, cot_all, y, c, csend, crecv, cpsend, cprecv)
    text_ring.begin()

    xcopies = []

    def deliver(block, kk):
        for dx in range(NX):
            wanted = sel_ref[kk * NX + dx]
            image = block[:LAT, :]
            for i in range(1, IMG):
                image = jnp.where(wanted == i, block[i * LAT : (i + 1) * LAT, :], image)
            if dx == 0:
                kv_ref[kk] = image
            else:
                picked[dx - 1, kk] = image
                copy = remote(
                    picked.at[dx - 1, kk],
                    kv_ref.at[dx * NZ + kk],
                    xsend.at[dx - 1, kk],
                    xrecv.at[dx - 1, kk],
                    {"x": lax.rem(x + dx, NX)},
                )
                copy.start()
                xcopies.append(copy)

    deliver(pairs_ref, 0)

    wcopies = []

    def send_weight(index):
        if index == 0:
            core, row = 1 - c, y
        else:
            row = lax.rem(y + (index + 1) // 2, NY)
            core = lax.rem(c + (index + 1) % 2, 2)
        columns = pl.ds(pl.multiple_of((2 * row + core) * 256, 256), 256)
        copy = remote(
            wo_ref.at[:, columns], wo_all.at[me], wsend.at[index], wrecv.at[index], {"y": row, "c": core}
        )
        copy.start()
        wcopies.append(copy)

    def own_weight():
        wo_all[me] = wo_ref[:, pl.ds(pl.multiple_of(me * 256, 256), 256)]

    todo = {}
    for k in range(1, HALF_Y + 1):
        todo.setdefault(2 * k - 1, []).append(functools.partial(text_ring.step, k))
        todo.setdefault(2 * k + 7, []).append(functools.partial(cot_ring.step, k))
    todo.setdefault(6, []).append(cot_ring.begin)
    todo.setdefault(6, []).append(own_weight)
    order = [7, 8, 9, 5, 6, 10, 3, 4, 11, 12, 1, 2, 13, 14, 0]
    for at, index in enumerate(order):
        todo.setdefault(4 + at // 2, []).append(functools.partial(send_weight, index))

    turn = 0
    for k in range(1, HALF_Z + 1):
        for ch in range(CHUNKS):
            for d in range(2):
                if exists(d, k, ch):
                    zcopies[d, k, ch].wait_recv()
                    if (d, k + 1, ch) in zcopies:
                        zcopies[d, k + 1, ch].start()
            for action in todo.get(turn, ()):
                action()
            turn += 1
        deliver(held[0][k], k)
        if k < HALF_Z:
            deliver(held[1][k], NZ - k)

    text_ring.finish()
    cot_ring.finish()
    for index in range(GROUP - 1):
        if index == 0:
            core, row = 1 - c, y
        else:
            row = lax.rem(y + NY - (index + 1) // 2, NY)
            core = lax.rem(c + (index + 1) % 2, 2)
        there = wo_all.at[2 * row + core]
        remote(there, there, wsend.at[index], wrecv.at[index], {"y": row, "c": core}).wait_recv()
    for copy in xcopies:
        copy.wait_recv()
    for copy in [*zcopies.values(), *xcopies, *wcopies]:
        copy.wait_send()


def gather_call(sel, pairs, text, cot, wo):
    vmem = pl.BlockSpec(memory_space=pltpu.VMEM)
    dma = pltpu.SemaphoreType.DMA
    ring = [dma((2, HALF_Y + 1)), dma((2, HALF_Y + 1)), dma((NY,)), dma((NY,))]
    return pl.pallas_call(
        gather_kernel,
        out_shape=(
            jax.ShapeDtypeStruct((NX * NZ, LAT, 256), BF16),
            jax.ShapeDtypeStruct((GROUP, TOK, 256), BF16),
            jax.ShapeDtypeStruct((GROUP, TOK, 256), BF16),
            jax.ShapeDtypeStruct((GROUP, 128, 256), BF16),
        ),
        in_specs=[pl.BlockSpec(memory_space=pltpu.SMEM)] + [vmem] * 4,
        out_specs=(vmem,) * 4,
        scratch_shapes=[
            pltpu.VMEM((NX - 1, NZ, LAT, 256), BF16),
            dma((2, HALF_Z + 1, CHUNKS)),
            dma((2, HALF_Z + 1, CHUNKS)),
            dma((NX - 1, NZ)),
            dma((NX - 1, NZ)),
            *ring,
            *ring,
            dma((GROUP - 1,)),
            dma((GROUP - 1,)),
        ]
        + [pltpu.VMEM((IMG * LAT, 256), BF16)] * (NZ - 1),
        compiler_params=pltpu.CompilerParams(
            collective_id=0, has_side_effects=True, vmem_limit_bytes=20 << 20
        ),
        name="gather_inputs",
    )(sel, pairs, text, cot, wo)


def attend_kernel(index_ref, text_all, wq_ref, gain_ref, bias_ref, kv_ref, pos_ref, ctx_ref):
    width = GROUP * 256
    total = jnp.zeros((TOK, 128), F32)
    for f in range(GROUP):
        block = text_all[f].astype(F32)
        total = total + block[:, :128] + block[:, 128:]
    mean = jnp.sum(total, axis=-1, keepdims=True) / width
    total = jnp.zeros((TOK, 128), F32)
    for f in range(GROUP):
        centered = text_all[f].astype(F32) - mean
        squared = centered * centered
        total = total + squared[:, :128] + squared[:, 128:]
    scale = lax.rsqrt(jnp.sum(total, axis=-1, keepdims=True) / width + EPSILON)
    acc = jnp.zeros((TOK, 128), F32)
    for f in range(GROUP):
        centered = text_all[f].astype(F32) - mean
        normed = (centered * scale * gain_ref[f : f + 1, :] + bias_ref[f : f + 1, :]).astype(BF16)
        acc = acc + jnp.dot(normed, wq_ref[f * 256 : (f + 1) * 256, :], preferred_element_type=F32)
    queries = (acc * 128 ** (-0.5)).astype(BF16)
    for s in range(3):
        rows = slice(s * LAT, (s + 1) * LAT)
        blocks = [kv_ref[index_ref[s * 5 + k]] for k in range(5)]
        keys = jnp.concatenate([b[:, :128] for b in blocks], axis=0)
        values = jnp.concatenate([b[:, 128:] for b in blocks], axis=0)
        scores = lax.dot_general(queries[rows], keys, (((1,), (1,)), ((), ())), preferred_element_type=F32)
        pos = pos_ref[rows, :]
        column = lax.broadcasted_iota(jnp.int32, scores.shape, 1) // LAT
        scores = jnp.where(pos == column, scores, -1e30)
        weights = jnp.exp(scores - jnp.max(scores, axis=-1, keepdims=True))
        probs = (weights / jnp.sum(weights, axis=-1, keepdims=True)).astype(BF16)
        context = jnp.dot(probs, values, preferred_element_type=F32)
        ctx_ref[rows, :] = jnp.where(pos >= 0, context, 0.0).astype(BF16)


def attend_call(index, text_all, wq, gain, bias, kv, pos):
    vmem = pl.BlockSpec(memory_space=pltpu.VMEM)
    return pl.pallas_call(
        attend_kernel,
        out_shape=jax.ShapeDtypeStruct((TOK, 128), BF16),
        in_specs=[pl.BlockSpec(memory_space=pltpu.SMEM)] + [vmem] * 6,
        out_specs=vmem,
        compiler_params=pltpu.CompilerParams(vmem_limit_bytes=16 << 20),
        name="attend",
    )(index, text_all, wq, gain, bias, kv, pos)


FAR_FIRST = [8, 7, 9, 6, 10, 5, 11, 4, 12, 3, 13, 2, 14, 1, 15, 0]


def combine_kernel(
    gate_ref,
    ctx_ref,
    cot_all,
    wo_all,
    text_ref,
    out_ref,
    grad_ref,
    product,
    own,
    gsend,
    grecv,
    hsend,
    hrecv,
    same,
    other,
    xs,
    xr,
    zs,
    zr,
    ys,
    yr,
    ps,
    pr,
):
    z, x, y, c = position()
    zpeers = [{"z": lax.rem(z + kk, NZ)} for kk in range(NZ)]
    xpeers = x_peers(x)
    ypeers = [{"y": lax.rem(y + dy, NY)} for dy in range(NY)]
    partner = {"c": 1 - c}
    meet([*zpeers[1:], *xpeers, *ypeers[1:], partner])()
    started = []

    def go(copy):
        copy.start()
        started.append(copy)
        return copy

    ycopies = {}
    for dy in (4, 3, 5, 2, 6, 1, 7):
        ycopies[dy] = go(remote(ctx_ref, same.at[dy], ys.at[dy], yr.at[dy], ypeers[dy]))
    pcopies = {0: go(remote(ctx_ref, other.at[0], ps.at[0], pr.at[0], partner))}

    context = ctx_ref[...]
    xcopies = {}
    for kk in FAR_FIRST:
        block = cot_all[lax.rem(z + kk, NZ)]
        product[kk] = lax.dot_general(block, context, (((0,), (0,)), ((), ())), preferred_element_type=F32)
        for dx in range(NX):
            rows = pl.ds(pl.multiple_of(lax.rem(x + dx, NX) * 64, 64), 64)
            part = product[kk, rows, :]
            if dx == 0:
                own[kk] = part
            else:
                gsend[dx - 1, kk] = part.astype(BF16)
                xcopies[dx, kk] = go(
                    remote(
                        gsend.at[dx - 1, kk],
                        grecv.at[dx - 1, kk],
                        xs.at[dx - 1, kk],
                        xr.at[dx - 1, kk],
                        xpeers[dx - 1],
                    )
                )
    def pass_on(dy):
        ycopies[dy].wait_recv()
        pcopies[dy] = go(remote(same.at[dy], other.at[dy], ps.at[dy], pr.at[dy], partner))

    near = [1, 7, 2, 6, 3, 5, 4]
    zcopies = {}
    for at, kk in enumerate(FAR_FIRST):
        total = own[kk]
        for dx in range(1, NX):
            xcopies[dx, kk].wait_recv()
            total = total + grecv[dx - 1, kk].astype(F32)
        if kk == 0:
            own[0] = total
        else:
            hsend[kk] = total.astype(BF16)
            zcopies[kk] = go(remote(hsend.at[kk], hrecv.at[kk], zs.at[kk], zr.at[kk], zpeers[kk]))
        if at % 2 == 1 and near:
            pass_on(near.pop(0))
    gate = gate_ref[0]
    update = jnp.zeros((TOK, 256), F32)
    for dy in (0, 1, 7, 2, 6, 3, 5, 4):
        row = 2 * lax.rem(y + NY - dy, NY)
        mine = context if dy == 0 else same[dy]
        update = update + jnp.dot(mine, wo_all[row + c], preferred_element_type=F32)
        pcopies[dy].wait_recv()
        update = update + jnp.dot(other[dy], wo_all[row + 1 - c], preferred_element_type=F32)
    out_ref[...] = (text_ref[...].astype(F32) + gate * update).astype(BF16)
    total = own[0]
    for kk in FAR_FIRST[::-1][1:]:
        zcopies[kk].wait_recv()
        total = total + hrecv[kk].astype(F32)
    grad_ref[...] = jnp.transpose(gate * total, (1, 0))
    for copy in started:
        copy.wait_send()


def combine_call(gate, ctx, cot_all, wo_all, text):
    vmem = pl.BlockSpec(memory_space=pltpu.VMEM)
    dma = pltpu.SemaphoreType.DMA
    return pl.pallas_call(
        combine_kernel,
        out_shape=(jax.ShapeDtypeStruct((TOK, 256), BF16), jax.ShapeDtypeStruct((128, 64), F32)),
        in_specs=[pl.BlockSpec(memory_space=pltpu.SMEM)] + [vmem] * 4,
        out_specs=(vmem, vmem),
        scratch_shapes=[
            pltpu.VMEM((NZ, 256, 128), F32),
            pltpu.VMEM((NZ, 64, 128), F32),
            pltpu.VMEM((NX - 1, NZ, 64, 128), BF16),
            pltpu.VMEM((NX - 1, NZ, 64, 128), BF16),
            pltpu.VMEM((NZ, 64, 128), BF16),
            pltpu.VMEM((NZ, 64, 128), BF16),
            pltpu.VMEM((NY, TOK, 128), BF16),
            pltpu.VMEM((NY, TOK, 128), BF16),
            dma((NX - 1, NZ)),
            dma((NX - 1, NZ)),
            dma((NZ,)),
            dma((NZ,)),
            dma((NY,)),
            dma((NY,)),
            dma((NY,)),
            dma((NY,)),
        ],
        compiler_params=pltpu.CompilerParams(
            collective_id=1, has_side_effects=True, vmem_limit_bytes=16 << 20
        ),
        name="combine_outputs",
    )(gate, ctx, cot_all, wo_all, text)


def routes(media_refs, owner_map, z, x):
    refs = lax.dynamic_slice_in_dim(media_refs.reshape(NZ, NX * 15), z, 1, 0).reshape(NX * 15)
    lookup = jnp.maximum(refs, 0)[:, None] == jnp.arange(owner_map.shape[0], dtype=jnp.int32)
    storage = jnp.sum(jnp.where(lookup, owner_map, 0), axis=-1)
    owner, within = storage // IMG, storage % IMG
    dz = (z + NZ - owner // NX) % NZ
    source_x = owner % NX
    dest_dx = (jnp.arange(NX * 15, dtype=jnp.int32) // 15 + NX - x) % NX
    cell = jnp.arange(NZ * NX, dtype=jnp.int32)[:, None]
    hit = (refs >= 0) & (source_x == x) & (dz * NX + dest_dx == cell)
    sel = jnp.sum(jnp.where(hit, within, 0), axis=-1)
    index = ((x + NX - source_x) % NX) * NZ + dz
    index = lax.dynamic_slice_in_dim(index, x * 15, 15, 0)
    return sel, index


def body(
    text_states,
    cotangent,
    norm_gain,
    norm_bias,
    branch_gate,
    query_weight,
    latent_weight,
    output_weight,
    latents,
    media_refs,
    media_pos,
    owner_map,
):
    z, x = lax.axis_index("z"), lax.axis_index("x")
    pairs = jnp.dot(
        latents.reshape(IMG * LAT, -1), latent_weight.reshape(-1, 256), preferred_element_type=F32
    ).astype(BF16)
    sel, index = routes(media_refs, owner_map, z, x)
    text = text_states.reshape(TOK, 256)
    kv, text_all, cot_all, wo_all = gather_call(
        sel, pairs, text, cotangent.reshape(TOK, 256), output_weight.reshape(128, -1)
    )
    context = attend_call(
        index,
        text_all,
        query_weight.reshape(-1, 128),
        norm_gain.reshape(GROUP, 256),
        norm_bias.reshape(GROUP, 256),
        kv,
        media_pos.reshape(TOK, 1),
    )
    layer_out, out_grad = combine_call(jnp.tanh(branch_gate), context, cot_all, wo_all, text)
    return layer_out.reshape(3, 64, 256), out_grad.reshape(1, 128, 64)


def solution(mesh):
    split = Mesh(mesh.devices.reshape(NZ, NX, NY, 2), ("z", "x", "y", "c"))
    dp, fsdp = ("z", "x"), ("y", "c")
    return jax.shard_map(
        body,
        mesh=split,
        in_specs=(
            P(dp, None, fsdp),
            P(dp, None, fsdp),
            P(),
            P(),
            P(),
            P(None, fsdp, None),
            P(None, fsdp, None),
            P(fsdp, None, None),
            P(dp, None, None),
            P(),
            P(dp, None),
            P(),
        ),
        out_specs=(P(dp, None, fsdp), P(fsdp, None, dp)),
        check_vma=False,
    )
```

```python
import functools

import jax
import jax.numpy as jnp
from jax import lax
from jax.experimental import pallas as pl
from jax.experimental.pallas import tpu as pltpu
from jax.sharding import Mesh
from jax.sharding import PartitionSpec as P

EPSILON = 1e-05
MESH = pl.DeviceIdType.MESH
NZ, NX, NY = 16, 4, 8
GROUP = 2 * NY
IMG = 9
LAT = 64
TOK = 192
CHUNKS = 3
CHUNK_ROWS = IMG * LAT // CHUNKS
QUARTER = 128 // NX
HALF_Z = NZ // 2
HALF_Y = NY // 2
BF16 = jnp.bfloat16
F32 = jnp.float32


def remote(src, dst, send, recv, where):
    return pltpu.make_async_remote_copy(
        src_ref=src, dst_ref=dst, send_sem=send, recv_sem=recv, device_id=where, device_id_type=MESH
    )


def position():
    return lax.axis_index("z"), lax.axis_index("x"), lax.axis_index("y"), lax.axis_index("c")


def meet(targets):
    barrier = pltpu.get_barrier_semaphore()
    for where in targets:
        pl.semaphore_signal(barrier, inc=1, device_id=where, device_id_type=MESH)
    return lambda: pl.semaphore_wait(barrier, len(targets))


def fsdp_peers(y, c):
    peers = [{"c": 1 - c}]
    for dy in range(1, NY):
        for dc in range(2):
            peers.append({"y": lax.rem(y + dy, NY), "c": lax.rem(c + dc, 2)})
    return peers


def x_peers(x):
    return [{"x": lax.rem(x + dx, NX)} for dx in range(1, NX)]


class YRing:
    def __init__(self, own, full, y, c, send, recv, psend, precv):
        self.own, self.full, self.y, self.c = own, full, y, c
        self.send, self.recv, self.psend, self.precv = send, recv, psend, precv
        self.started = []

    def slot(self, direction, k, core):
        row = lax.rem(self.y + (NY - k if direction == 0 else k), NY)
        return self.full.at[2 * row + core]

    def neighbour(self, direction):
        return {"y": lax.rem(self.y + (1 if direction == 0 else NY - 1), NY)}

    def hop(self, direction, k):
        src = self.own if k == 1 else self.slot(direction, k - 1, self.c)
        dst = self.slot(direction, k - 1, self.c)
        copy = remote(src, dst, self.send.at[direction, k], self.recv.at[direction, k], self.neighbour(direction))
        copy.start()
        self.started.append(copy)

    def to_partner(self, src, dst, index):
        copy = remote(src, dst, self.psend.at[index], self.precv.at[index], {"c": 1 - self.c})
        copy.start()
        self.started.append(copy)

    def begin(self):
        self.hop(0, 1)
        self.hop(1, 1)
        mine = self.slot(0, 0, self.c)
        self.to_partner(self.own, mine, 0)
        self.local = pltpu.make_async_copy(self.own, mine, self.psend.at[NY])
        self.local.start()

    def step(self, k):
        for direction, last in ((0, HALF_Y), (1, HALF_Y - 1)):
            if k <= last:
                here = self.slot(direction, k, self.c)
                remote(
                    here, here, self.send.at[direction, k], self.recv.at[direction, k], self.neighbour(direction)
                ).wait_recv()
                if k < last:
                    self.hop(direction, k + 1)
                self.to_partner(here, here, k + (HALF_Y if direction else 0))

    def finish(self):
        self.local.wait()
        for direction, last in ((0, HALF_Y), (1, HALF_Y - 1)):
            for k in range(0 if direction == 0 else 1, last + 1):
                index = k + (HALF_Y if direction else 0)
                there = self.slot(direction, k, 1 - self.c)
                remote(
                    there, there, self.psend.at[index], self.precv.at[index], {"c": 1 - self.c}
                ).wait_recv()
        for copy in self.started:
            copy.wait_send()


FAR_FIRST = [8, 7, 9, 6, 10, 5, 11, 4, 12, 3, 13, 2, 14, 1, 15, 0]


def fused_kernel(
    sel_ref,
    index_ref,
    gate_ref,
    latents_ref,
    wl_hbm,
    text_ref,
    cot_ref,
    wo_ref,
    wq_hbm,
    gain_ref,
    bias_ref,
    pos_ref,
    out_ref,
    grad_ref,
    wl_ref,
    wq_ref,
    lat,
    pairs_ref,
    kv_ref,
    text_all,
    cot_all,
    wo_all,
    picked,
    ctx_ref,
    product,
    own,
    gsend,
    grecv,
    hsend,
    hrecv,
    same,
    other,
    lsem,
    zsend,
    zrecv,
    xsend,
    xrecv,
    tsend,
    trecv,
    tpsend,
    tprecv,
    csend,
    crecv,
    cpsend,
    cprecv,
    wsend,
    wrecv,
    wxs,
    wxr,
    xs,
    xr,
    zs,
    zr,
    ys,
    yr,
    ps,
    pr,
    *slots,
):
    z, x, y, c = position()
    me = 2 * y + c
    ups = ({"z": lax.rem(z + 1, NZ)}, {"z": lax.rem(z + NZ - 1, NZ)})

    def chunk_rows(ch):
        return pl.ds(ch * CHUNK_ROWS, CHUNK_ROWS)

    loads = [
        pltpu.make_async_copy(latents_ref.at[chunk_rows(ch)], lat.at[chunk_rows(ch)], lsem.at[ch])
        for ch in range(CHUNKS)
    ]
    weight_load = pltpu.make_async_copy(wl_hbm, wl_ref, lsem.at[CHUNKS])
    query_load = pltpu.make_async_copy(wq_hbm, wq_ref, lsem.at[CHUNKS + 1])
    weight_load.start()
    for load in [*loads, query_load]:
        load.start()
    wait_peers = meet([*ups, *x_peers(x), *fsdp_peers(y, c)])
    started = []

    def go(copy):
        copy.start()
        started.append(copy)
        return copy

    held = ([pairs_ref, *slots[:HALF_Z]], [pairs_ref, *slots[HALF_Z:]] + [slots[HALF_Z - 1]])

    def exists(direction, k, ch):
        return k < HALF_Z or (k == HALF_Z and (ch == CHUNKS - 1) == (direction == 1))

    def zcopy(direction, k, ch):
        return remote(
            held[direction][k - 1].at[chunk_rows(ch)],
            held[direction][k].at[chunk_rows(ch)],
            zsend.at[direction, k, ch],
            zrecv.at[direction, k, ch],
            ups[direction],
        )

    zcopies = {}

    def hop(direction, k, ch):
        zcopies[direction, k, ch] = go(zcopy(direction, k, ch))

    text_ring = YRing(text_ref, text_all, y, c, tsend, trecv, tpsend, tprecv)
    cot_ring = YRing(cot_ref, cot_all, y, c, csend, crecv, cpsend, cprecv)

    weight_load.wait()
    for ch in range(CHUNKS):
        loads[ch].wait()
        pairs_ref[chunk_rows(ch), :] = jnp.dot(
            lat[chunk_rows(ch), :], wl_ref[...], preferred_element_type=F32
        ).astype(BF16)
        if ch == 0:
            wait_peers()
            text_ring.begin()
        for d in range(2):
            hop(d, 1, ch)

    xcopies = []

    def deliver(block, kk):
        for dx in (1, 2, 3, 0):
            wanted = sel_ref[kk * NX + dx]
            image = block[:LAT, :]
            for i in range(1, IMG):
                image = jnp.where(wanted == i, block[i * LAT : (i + 1) * LAT, :], image)
            if dx == 0:
                kv_ref[kk] = image
            else:
                picked[dx - 1, kk] = image
                xcopies.append(
                    go(
                        remote(
                            picked.at[dx - 1, kk],
                            kv_ref.at[dx * NZ + kk],
                            xsend.at[dx - 1, kk],
                            xrecv.at[dx - 1, kk],
                            {"x": lax.rem(x + dx, NX)},
                        )
                    )
                )

    def fsdp_place(index, sign):
        if index == 0:
            return y, 1 - c
        step = (index + 1) // 2
        row = lax.rem(y + (step if sign > 0 else NY - step), NY)
        return row, lax.rem(c + (index + 1) % 2, 2)

    quarter = pl.ds(pl.multiple_of(x * QUARTER, QUARTER), QUARTER)

    def weight_columns(row, core):
        return pl.ds(pl.multiple_of((2 * row + core) * 256, 256), 256)

    own_weight = pltpu.make_async_copy(
        wo_ref.at[quarter, weight_columns(y, c)], wo_all.at[me, quarter], lsem.at[CHUNKS + 2]
    )

    def send_weight(index):
        row, core = fsdp_place(index, 1)
        go(
            remote(
                wo_ref.at[quarter, weight_columns(row, core)],
                wo_all.at[me, quarter],
                wsend.at[index],
                wrecv.at[index],
                {"y": row, "c": core},
            )
        )

    def spread_weight():
        own_weight.wait()
        for index in range(GROUP - 1):
            row, core = fsdp_place(index, -1)
            there = wo_all.at[2 * row + core, quarter]
            remote(there, there, wsend.at[index], wrecv.at[index], {"y": row, "c": core}).wait_recv()
        for dx in range(1, NX):
            mine = wo_all.at[:, quarter]
            go(remote(mine, mine, wxs.at[dx], wxr.at[dx], {"x": lax.rem(x + dx, NX)}))

    def weight_spread():
        for dx in range(1, NX):
            rows = pl.ds(pl.multiple_of(lax.rem(x + NX - dx, NX) * QUARTER, QUARTER), QUARTER)
            there = wo_all.at[:, rows]
            remote(there, there, wxs.at[dx], wxr.at[dx], {"x": lax.rem(x + dx, NX)}).wait_recv()

    state = {}
    width = GROUP * 256

    def norm_mean():
        text_ring.finish()
        total = jnp.zeros((TOK, 128), F32)
        for f in range(GROUP):
            block = text_all[f].astype(F32)
            total = total + block[:, :128] + block[:, 128:]
        state["mean"] = jnp.sum(total, axis=-1, keepdims=True) / width

    def norm_scale():
        total = jnp.zeros((TOK, 128), F32)
        for f in range(GROUP):
            centered = text_all[f].astype(F32) - state["mean"]
            squared = centered * centered
            total = total + squared[:, :128] + squared[:, 128:]
        state["scale"] = lax.rsqrt(jnp.sum(total, axis=-1, keepdims=True) / width + EPSILON)

    def project(first, last):
        acc = state.get("acc", jnp.zeros((TOK, 128), F32))
        for f in range(first, last):
            centered = text_all[f].astype(F32) - state["mean"]
            normed = (centered * state["scale"] * gain_ref[:, f * 256 : (f + 1) * 256] + bias_ref[:, f * 256 : (f + 1) * 256]).astype(BF16)
            acc = acc + jnp.dot(normed, wq_ref[f * 256 : (f + 1) * 256, :], preferred_element_type=F32)
        state["acc"] = acc

    todo = {}

    def at_turn(turn, action, *args):
        todo.setdefault(turn, []).append(functools.partial(action, *args))

    for k in range(1, HALF_Y + 1):
        at_turn(2 * k - 1, text_ring.step, k)
        at_turn(2 * k + 10, cot_ring.step, k)
    at_turn(2, own_weight.start)
    for at, index in enumerate([7, 8, 9, 5, 6, 10, 3, 4, 11, 12, 1, 2, 13, 14, 0]):
        at_turn(4 + at // 4, send_weight, index)
    at_turn(7, cot_ring.begin)
    at_turn(9, query_load.wait)
    at_turn(10, norm_mean)
    at_turn(11, norm_scale)
    at_turn(13, project, 0, 8)
    at_turn(15, project, 8, 16)
    at_turn(14, spread_weight)

    deliver(pairs_ref, 0)
    turn = 0
    for k in range(1, HALF_Z + 1):
        for ch in range(CHUNKS):
            for d in range(2):
                if exists(d, k, ch):
                    zcopies[d, k, ch].wait_recv()
                    if k < HALF_Z and exists(d, k + 1, ch):
                        hop(d, k + 1, ch)
            for action in todo.get(turn, ()):
                action()
            turn += 1
        deliver(held[0][k], k)
        if k < HALF_Z:
            deliver(held[1][k], NZ - k)

    queries = (state["acc"] * 128 ** (-0.5)).astype(BF16)
    cot_ring.finish()
    for copy in xcopies:
        copy.wait_recv()
    square = (LAT, LAT)
    diagonal = lax.broadcasted_iota(jnp.int32, square, 0) == lax.broadcasted_iota(jnp.int32, square, 1)
    column = (lax.broadcasted_iota(jnp.int32, (LAT, 5 * LAT), 1) // LAT).astype(F32)
    for s in range(3):
        rows = slice(s * LAT, (s + 1) * LAT)
        blocks = [kv_ref[index_ref[k, 3 * x + s]] for k in range(5)]
        keys = jnp.concatenate([b[:, :128] for b in blocks], axis=0)
        values = jnp.concatenate([b[:, 128:] for b in blocks], axis=0)
        scores = lax.dot_general(queries[rows], keys, (((1,), (1,)), ((), ())), preferred_element_type=F32)
        pos = jnp.sum(jnp.where(diagonal, pos_ref[s : s + 1, :].astype(F32), 0.0), axis=1, keepdims=True)
        scores = jnp.where(pos == column, scores, -1e30)
        weights = jnp.exp(scores - jnp.max(scores, axis=-1, keepdims=True))
        probs = (weights / jnp.sum(weights, axis=-1, keepdims=True)).astype(BF16)
        mixed = jnp.dot(probs, values, preferred_element_type=F32)
        ctx_ref[rows, :] = jnp.where(pos >= 0, mixed, 0.0).astype(BF16)

    zpeers = [{"z": lax.rem(z + kk, NZ)} for kk in range(NZ)]
    xpeers = x_peers(x)
    partner = {"c": 1 - c}
    context = ctx_ref[...]
    gcopies = {}
    ycopies = {}
    pcopies = {}
    first = True
    for kk in FAR_FIRST:
        block = cot_all[lax.rem(z + kk, NZ)]
        product[kk] = lax.dot_general(block, context, (((0,), (0,)), ((), ())), preferred_element_type=F32)
        for dx in (1, 2, 3, 0):
            part = product[kk, pl.ds(pl.multiple_of(lax.rem(x + dx, NX) * 64, 64), 64), :]
            if dx == 0:
                own[kk] = part
            else:
                gsend[dx - 1, kk] = part.astype(BF16)
                gcopies[dx, kk] = go(
                    remote(
                        gsend.at[dx - 1, kk],
                        grecv.at[dx - 1, kk],
                        xs.at[dx - 1, kk],
                        xr.at[dx - 1, kk],
                        xpeers[dx - 1],
                    )
                )
        if first:
            first = False
            for dy in (4, 3, 5, 2, 6, 1, 7):
                ycopies[dy] = go(
                    remote(ctx_ref, same.at[dy], ys.at[dy], yr.at[dy], {"y": lax.rem(y + dy, NY)})
                )
            pcopies[0] = go(remote(ctx_ref, other.at[0], ps.at[0], pr.at[0], partner))

    def pass_on(dy):
        ycopies[dy].wait_recv()
        pcopies[dy] = go(remote(same.at[dy], other.at[dy], ps.at[dy], pr.at[dy], partner))

    near = [1, 7, 2, 6, 3, 5, 4]
    hcopies = {}
    for at, kk in enumerate(FAR_FIRST):
        total = own[kk]
        for dx in range(1, NX):
            gcopies[dx, kk].wait_recv()
            total = total + grecv[dx - 1, kk].astype(F32)
        if kk == 0:
            own[0] = total
        else:
            hsend[kk] = total.astype(BF16)
            hcopies[kk] = go(remote(hsend.at[kk], hrecv.at[kk], zs.at[kk], zr.at[kk], zpeers[kk]))
        if at % 2 == 1 and near:
            pass_on(near.pop(0))
    weight_spread()
    gate = gate_ref[0]
    update = jnp.zeros((TOK, 256), F32)
    for dy in (0, 1, 7, 2, 6, 3, 5, 4):
        row = 2 * lax.rem(y + NY - dy, NY)
        mine = context if dy == 0 else same[dy]
        update = update + jnp.dot(mine, wo_all[row + c], preferred_element_type=F32)
        pcopies[dy].wait_recv()
        update = update + jnp.dot(other[dy], wo_all[row + 1 - c], preferred_element_type=F32)
    out_ref[...] = (text_all[me].astype(F32) + gate * update).astype(BF16)
    total = own[0]
    for kk in FAR_FIRST[::-1][1:]:
        hcopies[kk].wait_recv()
        total = total + hrecv[kk].astype(F32)
    grad_ref[...] = gate * total
    for copy in started:
        copy.wait_send()


def fused_call(sel, index, gate, latents, wl, text, cot, wo, wq, gain, bias, pos):
    vmem = pl.BlockSpec(memory_space=pltpu.VMEM)
    smem = pl.BlockSpec(memory_space=pltpu.SMEM)
    dma = pltpu.SemaphoreType.DMA
    ring = [dma((2, HALF_Y + 1)), dma((2, HALF_Y + 1)), dma((NY + 1,)), dma((NY,))]
    return pl.pallas_call(
        fused_kernel,
        out_shape=(jax.ShapeDtypeStruct((TOK, 256), BF16), jax.ShapeDtypeStruct((64, 128), F32)),
        in_specs=[smem] * 3 + [pl.BlockSpec(memory_space=pltpu.HBM)] * 6 + [vmem] * 3,
        out_specs=(vmem, vmem),
        scratch_shapes=[
            pltpu.VMEM((GROUP * 256, 256), BF16),
            pltpu.VMEM((GROUP * 256, 128), BF16),
            pltpu.VMEM((IMG * LAT, GROUP * 256), BF16),
            pltpu.VMEM((IMG * LAT, 256), BF16),
            pltpu.VMEM((NX * NZ, LAT, 256), BF16),
            pltpu.VMEM((GROUP, TOK, 256), BF16),
            pltpu.VMEM((GROUP, TOK, 256), BF16),
            pltpu.VMEM((GROUP, 128, 256), BF16),
            pltpu.VMEM((NX - 1, NZ, LAT, 256), BF16),
            pltpu.VMEM((TOK, 128), BF16),
            pltpu.VMEM((NZ, 256, 128), F32),
            pltpu.VMEM((NZ, 64, 128), F32),
            pltpu.VMEM((NX - 1, NZ, 64, 128), BF16),
            pltpu.VMEM((NX - 1, NZ, 64, 128), BF16),
            pltpu.VMEM((NZ, 64, 128), BF16),
            pltpu.VMEM((NZ, 64, 128), BF16),
            pltpu.VMEM((NY, TOK, 128), BF16),
            pltpu.VMEM((NY, TOK, 128), BF16),
            dma((CHUNKS + 3,)),
            dma((2, HALF_Z + 1, CHUNKS)),
            dma((2, HALF_Z + 1, CHUNKS)),
            dma((NX - 1, NZ)),
            dma((NX - 1, NZ)),
            *ring,
            *ring,
            dma((GROUP - 1,)),
            dma((GROUP - 1,)),
            dma((NX,)),
            dma((NX,)),
            dma((NX - 1, NZ)),
            dma((NX - 1, NZ)),
            dma((NZ,)),
            dma((NZ,)),
            dma((NY,)),
            dma((NY,)),
            dma((NY,)),
            dma((NY,)),
        ]
        + [pltpu.VMEM((IMG * LAT, 256), BF16)] * (NZ - 1),
        compiler_params=pltpu.CompilerParams(
            collective_id=0, has_side_effects=True, vmem_limit_bytes=62 << 20
        ),
        name="fused",
    )(sel, index, gate, latents, wl, text, cot, wo, wq, gain, bias, pos)


def routes(media_refs, owner_map, z, x):
    refs = lax.dynamic_slice_in_dim(media_refs.T, 12 * z, 12, 1)
    lookup = jnp.maximum(refs, 0)[:, :, None] == jnp.arange(owner_map.shape[0], dtype=jnp.int32)
    storage = jnp.sum(jnp.where(lookup, owner_map, 0), axis=-1)
    owner, within = storage // IMG, storage % IMG
    dz = (z + NZ - owner // NX) % NZ
    source_x = owner % NX
    dest_dx = (jnp.arange(12, dtype=jnp.int32) // 3 + NX - x) % NX
    cell = jnp.arange(NZ * NX, dtype=jnp.int32)[:, None, None]
    hit = (refs >= 0) & (source_x == x) & (dz * NX + dest_dx == cell)
    sel = jnp.sum(jnp.where(hit, within, 0), axis=(1, 2))
    index = ((x + NX - source_x) % NX) * NZ + dz
    return sel, index


def body(
    text_states,
    cotangent,
    norm_gain,
    norm_bias,
    branch_gate,
    query_weight,
    latent_weight,
    output_weight,
    latents,
    media_refs,
    media_pos,
    owner_map,
):
    sel, index = routes(media_refs, owner_map, lax.axis_index("z"), lax.axis_index("x"))
    layer_out, out_grad = fused_call(
        sel,
        index,
        jnp.tanh(branch_gate),
        latents.reshape(IMG * LAT, -1),
        latent_weight.reshape(-1, 256),
        text_states.reshape(TOK, 256),
        cotangent.reshape(TOK, 256),
        output_weight.reshape(128, -1),
        query_weight.reshape(-1, 128),
        norm_gain.reshape(1, -1),
        norm_bias.reshape(1, -1),
        media_pos,
    )
    return layer_out.reshape(3, 64, 256), jnp.transpose(out_grad, (1, 0))[None]


def solution(mesh):
    split = Mesh(mesh.devices.reshape(NZ, NX, NY, 2), ("z", "x", "y", "c"))
    dp, fsdp = ("z", "x"), ("y", "c")
    return jax.shard_map(
        body,
        mesh=split,
        in_specs=(
            P(dp, None, fsdp),
            P(dp, None, fsdp),
            P(),
            P(),
            P(),
            P(None, fsdp, None),
            P(None, fsdp, None),
            P(fsdp, None, None),
            P(dp, None, None),
            P(),
            P(dp, None),
            P(),
        ),
        out_specs=(P(dp, None, fsdp), P(fsdp, None, dp)),
        check_vma=False,
    )
```

```python
import functools

import jax
import jax.numpy as jnp
from jax import lax
from jax.experimental import pallas as pl
from jax.experimental.pallas import tpu as pltpu
from jax.sharding import Mesh
from jax.sharding import PartitionSpec as P

EPSILON = 1e-05
MESH = pl.DeviceIdType.MESH
NZ, NX, NY = 16, 4, 8
GROUP = 2 * NY
IMG = 9
LAT = 64
TOK = 192
CHUNKS = 3
CHUNK_IMG = IMG // CHUNKS
CHUNK_ROWS = CHUNK_IMG * LAT
QUARTER = 128 // NX
HALF_Z = NZ // 2
HALF_Y = NY // 2
BF16 = jnp.bfloat16
F32 = jnp.float32


def remote(src, dst, send, recv, where):
    return pltpu.make_async_remote_copy(
        src_ref=src, dst_ref=dst, send_sem=send, recv_sem=recv, device_id=where, device_id_type=MESH
    )


def position():
    return lax.axis_index("z"), lax.axis_index("x"), lax.axis_index("y"), lax.axis_index("c")


def meet(targets):
    barrier = pltpu.get_barrier_semaphore()
    for where in targets:
        pl.semaphore_signal(barrier, inc=1, device_id=where, device_id_type=MESH)
    return lambda: pl.semaphore_wait(barrier, len(targets))


def fsdp_peers(y, c):
    peers = [{"c": 1 - c}]
    for dy in range(1, NY):
        for dc in range(2):
            peers.append({"y": lax.rem(y + dy, NY), "c": lax.rem(c + dc, 2)})
    return peers


def x_peers(x):
    return [{"x": lax.rem(x + dx, NX)} for dx in range(1, NX)]


class YRing:
    def __init__(self, own, full, y, c, send, recv, psend, precv):
        self.own, self.full, self.y, self.c = own, full, y, c
        self.send, self.recv, self.psend, self.precv = send, recv, psend, precv
        self.started = []

    def slot(self, direction, k, core):
        row = lax.rem(self.y + (NY - k if direction == 0 else k), NY)
        return self.full.at[2 * row + core]

    def neighbour(self, direction):
        return {"y": lax.rem(self.y + (1 if direction == 0 else NY - 1), NY)}

    def hop(self, direction, k):
        src = self.own if k == 1 else self.slot(direction, k - 1, self.c)
        dst = self.slot(direction, k - 1, self.c)
        copy = remote(src, dst, self.send.at[direction, k], self.recv.at[direction, k], self.neighbour(direction))
        copy.start()
        self.started.append(copy)

    def to_partner(self, src, dst, index):
        copy = remote(src, dst, self.psend.at[index], self.precv.at[index], {"c": 1 - self.c})
        copy.start()
        self.started.append(copy)

    def begin(self):
        self.hop(0, 1)
        self.hop(1, 1)
        mine = self.slot(0, 0, self.c)
        self.to_partner(self.own, mine, 0)
        self.local = pltpu.make_async_copy(self.own, mine, self.psend.at[NY])
        self.local.start()

    def step(self, k):
        for direction, last in ((0, HALF_Y), (1, HALF_Y - 1)):
            if k <= last:
                here = self.slot(direction, k, self.c)
                remote(
                    here, here, self.send.at[direction, k], self.recv.at[direction, k], self.neighbour(direction)
                ).wait_recv()
                if k < last:
                    self.hop(direction, k + 1)
                self.to_partner(here, here, k + (HALF_Y if direction else 0))

    def finish(self):
        self.local.wait()
        for direction, last in ((0, HALF_Y), (1, HALF_Y - 1)):
            for k in range(0 if direction == 0 else 1, last + 1):
                index = k + (HALF_Y if direction else 0)
                there = self.slot(direction, k, 1 - self.c)
                remote(
                    there, there, self.psend.at[index], self.precv.at[index], {"c": 1 - self.c}
                ).wait_recv()
        for copy in self.started:
            copy.wait_send()


FAR_FIRST = [8, 7, 9, 6, 10, 5, 11, 4, 12, 3, 13, 2, 14, 1, 15, 0]


def fused_kernel(
    refs_ref,
    owner_ref,
    gate_ref,
    latents_ref,
    wl_hbm,
    text_ref,
    cot_ref,
    wo_ref,
    wq_hbm,
    gain_ref,
    bias_ref,
    pos_ref,
    out_ref,
    grad_ref,
    wl_ref,
    wq_ref,
    lat,
    pairs_ref,
    kv_ref,
    text_all,
    cot_all,
    wo_all,
    picked,
    far_picked,
    stored,
    ctx_ref,
    product,
    own,
    gsend,
    grecv,
    hsend,
    hrecv,
    same,
    other,
    lsem,
    zsend,
    zrecv,
    xsend,
    xrecv,
    fsend,
    frecv,
    tsend,
    trecv,
    tpsend,
    tprecv,
    csend,
    crecv,
    cpsend,
    cprecv,
    wsend,
    wrecv,
    wxs,
    wxr,
    xs,
    xr,
    zs,
    zr,
    ys,
    yr,
    ps,
    pr,
    *slots,
):
    z, x, y, c = position()
    me = 2 * y + c
    ups = ({"z": lax.rem(z + 1, NZ)}, {"z": lax.rem(z + NZ - 1, NZ)})

    def chunk_rows(ch):
        return pl.ds(ch * CHUNK_ROWS, CHUNK_ROWS)

    loads = [
        pltpu.make_async_copy(latents_ref.at[chunk_rows(ch)], lat.at[chunk_rows(ch)], lsem.at[ch])
        for ch in range(CHUNKS)
    ]
    weight_load = pltpu.make_async_copy(wl_hbm, wl_ref, lsem.at[CHUNKS])
    query_load = pltpu.make_async_copy(wq_hbm, wq_ref, lsem.at[CHUNKS + 1])
    weight_load.start()
    for load in [*loads, query_load]:
        load.start()
    wait_peers = meet([*ups, *x_peers(x), *fsdp_peers(y, c)])
    started = []

    def go(copy):
        copy.start()
        started.append(copy)
        return copy

    held = ([pairs_ref, *slots[: HALF_Z - 1]], [pairs_ref, *slots[HALF_Z - 1 :]])

    def zcopy(direction, k, ch):
        images = pl.ds(ch * CHUNK_IMG, CHUNK_IMG)
        return remote(
            held[direction][k - 1].at[images],
            held[direction][k].at[images],
            zsend.at[direction, k, ch],
            zrecv.at[direction, k, ch],
            ups[direction],
        )

    def find(place, plane, dx):
        first = 3 * (NX * plane + lax.rem(x + dx, NX))
        for s in range(3):
            for k in range(5):
                ref = refs_ref[k, first + s]
                row = owner_ref[jnp.maximum(ref, 0)]
                stored[place * 15 + s * 5 + k] = jnp.where(ref >= 0, row, -1000)

    def within(place, plane):
        base = IMG * (NX * plane + x)
        wanted = 0
        for e in range(15):
            at = stored[place * 15 + e] - base
            wanted = wanted + jnp.where((at >= 0) & (at < IMG), at, 0)
        return wanted

    zcopies = {}

    def hop(direction, k, ch):
        zcopies[direction, k, ch] = go(zcopy(direction, k, ch))

    text_ring = YRing(text_ref, text_all, y, c, tsend, trecv, tpsend, tprecv)
    cot_ring = YRing(cot_ref, cot_all, y, c, csend, crecv, cpsend, cprecv)

    for dx in range(NX):
        find(dx, z, dx)
    weight_load.wait()
    for ch in range(CHUNKS):
        loads[ch].wait()
        pairs_ref[ch * CHUNK_IMG : (ch + 1) * CHUNK_IMG] = (
            jnp.dot(lat[chunk_rows(ch), :], wl_ref[...], preferred_element_type=F32)
            .astype(BF16)
            .reshape(CHUNK_IMG, LAT, 256)
        )
        if ch == 0:
            wait_peers()
            text_ring.begin()
        for d in range(2):
            hop(d, 1, ch)

    xcopies = []

    def deliver(block, kk):
        for dx in (1, 2, 3, 0):
            image = block[within(dx, lax.rem(z + NZ - kk, NZ))]
            if dx == 0:
                kv_ref[kk] = image
            else:
                picked[dx - 1, kk] = image
                xcopies.append(
                    go(
                        remote(
                            picked.at[dx - 1, kk],
                            kv_ref.at[dx * NZ + kk],
                            xsend.at[dx - 1, kk],
                            xrecv.at[dx - 1, kk],
                            {"x": lax.rem(x + dx, NX)},
                        )
                    )
                )

    far_up, far_down = lax.rem(z + NZ - HALF_Z + 1, NZ), lax.rem(z + HALF_Z - 1, NZ)
    far = [(1, 0, far_up), (2, 0, far_up), (3, 1, far_down), (0, 1, far_down)]
    far_copies = []

    def find_far():
        for dx, direction, _ in far:
            find(NX + dx, ups[direction]["z"], dx)

    def deliver_far():
        for dx, direction, source in far:
            far_picked[dx] = held[direction][HALF_Z - 1][within(NX + dx, source)]
            where = {"z": ups[direction]["z"], "x": lax.rem(x + dx, NX)}
            far_copies.append(
                go(
                    remote(
                        far_picked.at[dx],
                        kv_ref.at[dx * NZ + HALF_Z],
                        fsend.at[dx],
                        frecv.at[dx],
                        where if dx else ups[direction],
                    )
                )
            )

    def fsdp_place(index, sign):
        if index == 0:
            return y, 1 - c
        step = (index + 1) // 2
        row = lax.rem(y + (step if sign > 0 else NY - step), NY)
        return row, lax.rem(c + (index + 1) % 2, 2)

    quarter = pl.ds(pl.multiple_of(x * QUARTER, QUARTER), QUARTER)

    def weight_columns(row, core):
        return pl.ds(pl.multiple_of((2 * row + core) * 256, 256), 256)

    own_weight = pltpu.make_async_copy(
        wo_ref.at[quarter, weight_columns(y, c)], wo_all.at[me, quarter], lsem.at[CHUNKS + 2]
    )

    def send_weight(index):
        row, core = fsdp_place(index, 1)
        go(
            remote(
                wo_ref.at[quarter, weight_columns(row, core)],
                wo_all.at[me, quarter],
                wsend.at[index],
                wrecv.at[index],
                {"y": row, "c": core},
            )
        )

    def spread_weight():
        own_weight.wait()
        for index in range(GROUP - 1):
            row, core = fsdp_place(index, -1)
            there = wo_all.at[2 * row + core, quarter]
            remote(there, there, wsend.at[index], wrecv.at[index], {"y": row, "c": core}).wait_recv()
        for dx in range(1, NX):
            mine = wo_all.at[:, quarter]
            go(remote(mine, mine, wxs.at[dx], wxr.at[dx], {"x": lax.rem(x + dx, NX)}))

    def weight_spread():
        for dx in range(1, NX):
            rows = pl.ds(pl.multiple_of(lax.rem(x + NX - dx, NX) * QUARTER, QUARTER), QUARTER)
            there = wo_all.at[:, rows]
            remote(there, there, wxs.at[dx], wxr.at[dx], {"x": lax.rem(x + dx, NX)}).wait_recv()

    state = {}
    width = GROUP * 256

    def norm_mean():
        text_ring.finish()
        total = jnp.zeros((TOK, 128), F32)
        for f in range(GROUP):
            block = text_all[f].astype(F32)
            total = total + block[:, :128] + block[:, 128:]
        state["mean"] = jnp.sum(total, axis=-1, keepdims=True) / width

    def norm_scale():
        total = jnp.zeros((TOK, 128), F32)
        for f in range(GROUP):
            centered = text_all[f].astype(F32) - state["mean"]
            squared = centered * centered
            total = total + squared[:, :128] + squared[:, 128:]
        state["scale"] = lax.rsqrt(jnp.sum(total, axis=-1, keepdims=True) / width + EPSILON)

    def project(first, last):
        acc = state.get("acc", jnp.zeros((TOK, 128), F32))
        for f in range(first, last):
            centered = text_all[f].astype(F32) - state["mean"]
            normed = (centered * state["scale"] * gain_ref[:, f * 256 : (f + 1) * 256] + bias_ref[:, f * 256 : (f + 1) * 256]).astype(BF16)
            acc = acc + jnp.dot(normed, wq_ref[f * 256 : (f + 1) * 256, :], preferred_element_type=F32)
        state["acc"] = acc

    todo = {}

    def at_turn(turn, action, *args):
        todo.setdefault(turn, []).append(functools.partial(action, *args))

    for k in range(1, HALF_Y + 1):
        at_turn(2 * k - 1, text_ring.step, k)
        at_turn(2 * k + 10, cot_ring.step, k)
    at_turn(2, own_weight.start)
    for at, index in enumerate([7, 8, 9, 5, 6, 10, 3, 4, 11, 12, 1, 2, 13, 14, 0]):
        at_turn(4 + at // 4, send_weight, index)
    at_turn(7, cot_ring.begin)
    at_turn(9, query_load.wait)
    at_turn(10, norm_mean)
    at_turn(11, norm_scale)
    at_turn(13, project, 0, 8)
    at_turn(15, project, 8, 16)
    at_turn(14, spread_weight)

    at_turn(16, find_far)
    deliver(pairs_ref, 0)
    turn = 0
    for k in range(1, HALF_Z):
        for ch in range(CHUNKS):
            for d in range(2):
                zcopies[d, k, ch].wait_recv()
                if k < HALF_Z - 1:
                    hop(d, k + 1, ch)
            for action in todo.get(turn, ()):
                action()
            turn += 1
        if k == HALF_Z - 1:
            deliver_far()
        deliver(held[0][k], k)
        deliver(held[1][k], NZ - k)

    queries = (state["acc"] * 128 ** (-0.5)).astype(BF16)
    cot_ring.finish()
    for copy in [*xcopies, *far_copies]:
        copy.wait_recv()

    def arrival(entry):
        owner = lax.div(jnp.maximum(stored[entry], 0), IMG)
        from_x = lax.rem(x + NX - lax.rem(owner, NX), NX)
        return from_x * NZ + lax.rem(z + NZ - lax.div(owner, NX), NZ)

    square = (LAT, LAT)
    diagonal = lax.broadcasted_iota(jnp.int32, square, 0) == lax.broadcasted_iota(jnp.int32, square, 1)
    column = (lax.broadcasted_iota(jnp.int32, (LAT, 5 * LAT), 1) // LAT).astype(F32)
    for s in range(3):
        rows = slice(s * LAT, (s + 1) * LAT)
        blocks = [kv_ref[arrival(s * 5 + k)] for k in range(5)]
        keys = jnp.concatenate([b[:, :128] for b in blocks], axis=0)
        values = jnp.concatenate([b[:, 128:] for b in blocks], axis=0)
        scores = lax.dot_general(queries[rows], keys, (((1,), (1,)), ((), ())), preferred_element_type=F32)
        pos = jnp.sum(jnp.where(diagonal, pos_ref[s : s + 1, :].astype(F32), 0.0), axis=1, keepdims=True)
        scores = jnp.where(pos == column, scores, -1e30)
        weights = jnp.exp(scores - jnp.max(scores, axis=-1, keepdims=True))
        probs = (weights / jnp.sum(weights, axis=-1, keepdims=True)).astype(BF16)
        mixed = jnp.dot(probs, values, preferred_element_type=F32)
        ctx_ref[rows, :] = jnp.where(pos >= 0, mixed, 0.0).astype(BF16)

    zpeers = [{"z": lax.rem(z + kk, NZ)} for kk in range(NZ)]
    xpeers = x_peers(x)
    partner = {"c": 1 - c}
    context = ctx_ref[...]
    gcopies = {}
    ycopies = {}
    pcopies = {}
    first = True
    for kk in FAR_FIRST:
        block = cot_all[lax.rem(z + kk, NZ)]
        product[kk] = lax.dot_general(block, context, (((0,), (0,)), ((), ())), preferred_element_type=F32)
        for dx in (1, 2, 3, 0):
            part = product[kk, pl.ds(pl.multiple_of(lax.rem(x + dx, NX) * 64, 64), 64), :]
            if dx == 0:
                own[kk] = part
            else:
                gsend[dx - 1, kk] = part.astype(BF16)
                gcopies[dx, kk] = go(
                    remote(
                        gsend.at[dx - 1, kk],
                        grecv.at[dx - 1, kk],
                        xs.at[dx - 1, kk],
                        xr.at[dx - 1, kk],
                        xpeers[dx - 1],
                    )
                )
        if first:
            first = False
            for dy in (4, 3, 5, 2, 6, 1, 7):
                ycopies[dy] = go(
                    remote(ctx_ref, same.at[dy], ys.at[dy], yr.at[dy], {"y": lax.rem(y + dy, NY)})
                )
            pcopies[0] = go(remote(ctx_ref, other.at[0], ps.at[0], pr.at[0], partner))

    def pass_on(dy):
        ycopies[dy].wait_recv()
        pcopies[dy] = go(remote(same.at[dy], other.at[dy], ps.at[dy], pr.at[dy], partner))

    near = [1, 7, 2, 6, 3, 5, 4]
    hcopies = {}
    for at, kk in enumerate(FAR_FIRST):
        total = own[kk]
        for dx in range(1, NX):
            gcopies[dx, kk].wait_recv()
            total = total + grecv[dx - 1, kk].astype(F32)
        if kk == 0:
            own[0] = total
        else:
            hsend[kk] = total.astype(BF16)
            hcopies[kk] = go(remote(hsend.at[kk], hrecv.at[kk], zs.at[kk], zr.at[kk], zpeers[kk]))
        if at % 2 == 1 and near:
            pass_on(near.pop(0))
    weight_spread()
    gate = gate_ref[0]
    update = jnp.zeros((TOK, 256), F32)
    for dy in (0, 1, 7, 2, 6, 3, 5, 4):
        row = 2 * lax.rem(y + NY - dy, NY)
        mine = context if dy == 0 else same[dy]
        update = update + jnp.dot(mine, wo_all[row + c], preferred_element_type=F32)
        pcopies[dy].wait_recv()
        update = update + jnp.dot(other[dy], wo_all[row + 1 - c], preferred_element_type=F32)
    out_ref[...] = (text_all[me].astype(F32) + gate * update).astype(BF16)
    total = own[0]
    for kk in FAR_FIRST[::-1][1:]:
        hcopies[kk].wait_recv()
        total = total + hrecv[kk].astype(F32)
    grad_ref[...] = gate * total
    for copy in started:
        copy.wait_send()


def fused_call(refs, owner, gate, latents, wl, text, cot, wo, wq, gain, bias, pos):
    vmem = pl.BlockSpec(memory_space=pltpu.VMEM)
    smem = pl.BlockSpec(memory_space=pltpu.SMEM)
    dma = pltpu.SemaphoreType.DMA
    ring = [dma((2, HALF_Y + 1)), dma((2, HALF_Y + 1)), dma((NY + 1,)), dma((NY,))]
    return pl.pallas_call(
        fused_kernel,
        out_shape=(jax.ShapeDtypeStruct((TOK, 256), BF16), jax.ShapeDtypeStruct((64, 128), F32)),
        in_specs=[smem] * 3 + [pl.BlockSpec(memory_space=pltpu.HBM)] * 6 + [vmem] * 3,
        out_specs=(vmem, vmem),
        scratch_shapes=[
            pltpu.VMEM((GROUP * 256, 256), BF16),
            pltpu.VMEM((GROUP * 256, 128), BF16),
            pltpu.VMEM((IMG * LAT, GROUP * 256), BF16),
            pltpu.VMEM((IMG, LAT, 256), BF16),
            pltpu.VMEM((NX * NZ, LAT, 256), BF16),
            pltpu.VMEM((GROUP, TOK, 256), BF16),
            pltpu.VMEM((GROUP, TOK, 256), BF16),
            pltpu.VMEM((GROUP, 128, 256), BF16),
            pltpu.VMEM((NX - 1, NZ, LAT, 256), BF16),
            pltpu.VMEM((NX, LAT, 256), BF16),
            pltpu.SMEM((2 * NX * 15,), jnp.int32),
            pltpu.VMEM((TOK, 128), BF16),
            pltpu.VMEM((NZ, 256, 128), F32),
            pltpu.VMEM((NZ, 64, 128), F32),
            pltpu.VMEM((NX - 1, NZ, 64, 128), BF16),
            pltpu.VMEM((NX - 1, NZ, 64, 128), BF16),
            pltpu.VMEM((NZ, 64, 128), BF16),
            pltpu.VMEM((NZ, 64, 128), BF16),
            pltpu.VMEM((NY, TOK, 128), BF16),
            pltpu.VMEM((NY, TOK, 128), BF16),
            dma((CHUNKS + 3,)),
            dma((2, HALF_Z, CHUNKS)),
            dma((2, HALF_Z, CHUNKS)),
            dma((NX - 1, NZ)),
            dma((NX - 1, NZ)),
            dma((NX,)),
            dma((NX,)),
            *ring,
            *ring,
            dma((GROUP - 1,)),
            dma((GROUP - 1,)),
            dma((NX,)),
            dma((NX,)),
            dma((NX - 1, NZ)),
            dma((NX - 1, NZ)),
            dma((NZ,)),
            dma((NZ,)),
            dma((NY,)),
            dma((NY,)),
            dma((NY,)),
            dma((NY,)),
        ]
        + [pltpu.VMEM((IMG, LAT, 256), BF16)] * (2 * (HALF_Z - 1)),
        compiler_params=pltpu.CompilerParams(
            collective_id=0, has_side_effects=True, vmem_limit_bytes=62 << 20
        ),
        name="fused",
    )(refs, owner, gate, latents, wl, text, cot, wo, wq, gain, bias, pos)


def body(
    text_states,
    cotangent,
    norm_gain,
    norm_bias,
    branch_gate,
    query_weight,
    latent_weight,
    output_weight,
    latents,
    media_refs,
    media_pos,
    owner_map,
):
    layer_out, out_grad = fused_call(
        media_refs.T,
        owner_map,
        jnp.tanh(branch_gate),
        latents.reshape(IMG * LAT, -1),
        latent_weight.reshape(-1, 256),
        text_states.reshape(TOK, 256),
        cotangent.reshape(TOK, 256),
        output_weight.reshape(128, -1),
        query_weight.reshape(-1, 128),
        norm_gain.reshape(1, -1),
        norm_bias.reshape(1, -1),
        media_pos,
    )
    return layer_out.reshape(3, 64, 256), jnp.transpose(out_grad, (1, 0))[None]


def solution(mesh):
    split = Mesh(mesh.devices.reshape(NZ, NX, NY, 2), ("z", "x", "y", "c"))
    dp, fsdp = ("z", "x"), ("y", "c")
    return jax.shard_map(
        body,
        mesh=split,
        in_specs=(
            P(dp, None, fsdp),
            P(dp, None, fsdp),
            P(),
            P(),
            P(),
            P(None, fsdp, None),
            P(None, fsdp, None),
            P(fsdp, None, None),
            P(dp, None, None),
            P(),
            P(dp, None),
            P(),
        ),
        out_specs=(P(dp, None, fsdp), P(fsdp, None, dp)),
        check_vma=False,
    )
```

```python
import functools

import jax
import jax.numpy as jnp
from jax import lax
from jax.experimental import pallas as pl
from jax.experimental.pallas import tpu as pltpu
from jax.sharding import Mesh
from jax.sharding import PartitionSpec as P

EPSILON = 1e-05
MESH = pl.DeviceIdType.MESH
NZ, NX, NY = 16, 4, 8
GROUP = 2 * NY
IMG = 9
LAT = 64
TOK = 192
CHUNKS = 3
CHUNK_IMG = IMG // CHUNKS
CHUNK_ROWS = CHUNK_IMG * LAT
QUARTER = 128 // NX
HALF_Z = NZ // 2
HALF_Y = NY // 2
BF16 = jnp.bfloat16
F32 = jnp.float32


def remote(src, dst, send, recv, where):
    return pltpu.make_async_remote_copy(
        src_ref=src, dst_ref=dst, send_sem=send, recv_sem=recv, device_id=where, device_id_type=MESH
    )


def position():
    return lax.axis_index("z"), lax.axis_index("x"), lax.axis_index("y"), lax.axis_index("c")


def meet(targets):
    barrier = pltpu.get_barrier_semaphore()
    for where in targets:
        pl.semaphore_signal(barrier, inc=1, device_id=where, device_id_type=MESH)
    return lambda: pl.semaphore_wait(barrier, len(targets))


def fsdp_peers(y, c):
    peers = [{"c": 1 - c}]
    for dy in range(1, NY):
        for dc in range(2):
            peers.append({"y": lax.rem(y + dy, NY), "c": lax.rem(c + dc, 2)})
    return peers


def x_peers(x):
    return [{"x": lax.rem(x + dx, NX)} for dx in range(1, NX)]


class YRing:
    def __init__(self, own, full, y, c, send, recv, psend, precv):
        self.own, self.full, self.y, self.c = own, full, y, c
        self.send, self.recv, self.psend, self.precv = send, recv, psend, precv
        self.started = []

    def slot(self, direction, k, core):
        row = lax.rem(self.y + (NY - k if direction == 0 else k), NY)
        return self.full.at[2 * row + core]

    def neighbour(self, direction):
        return {"y": lax.rem(self.y + (1 if direction == 0 else NY - 1), NY)}

    def hop(self, direction, k):
        src = self.own if k == 1 else self.slot(direction, k - 1, self.c)
        dst = self.slot(direction, k - 1, self.c)
        copy = remote(src, dst, self.send.at[direction, k], self.recv.at[direction, k], self.neighbour(direction))
        copy.start()
        self.started.append(copy)

    def to_partner(self, src, dst, index):
        copy = remote(src, dst, self.psend.at[index], self.precv.at[index], {"c": 1 - self.c})
        copy.start()
        self.started.append(copy)

    def begin(self):
        self.hop(0, 1)
        self.hop(1, 1)
        mine = self.slot(0, 0, self.c)
        self.to_partner(self.own, mine, 0)
        self.local = pltpu.make_async_copy(self.own, mine, self.psend.at[NY])
        self.local.start()

    def step(self, k):
        for direction, last in ((0, HALF_Y), (1, HALF_Y - 1)):
            if k <= last:
                here = self.slot(direction, k, self.c)
                remote(
                    here, here, self.send.at[direction, k], self.recv.at[direction, k], self.neighbour(direction)
                ).wait_recv()
                if k < last:
                    self.hop(direction, k + 1)
                self.to_partner(here, here, k + (HALF_Y if direction else 0))

    def finish(self):
        self.local.wait()
        for direction, last in ((0, HALF_Y), (1, HALF_Y - 1)):
            for k in range(0 if direction == 0 else 1, last + 1):
                index = k + (HALF_Y if direction else 0)
                there = self.slot(direction, k, 1 - self.c)
                remote(
                    there, there, self.psend.at[index], self.precv.at[index], {"c": 1 - self.c}
                ).wait_recv()
        for copy in self.started:
            copy.wait_send()


FAR_FIRST = [8, 7, 9, 6, 10, 5, 11, 4, 12, 3, 13, 2, 14, 1, 15, 0]


def fused_kernel(
    refs_ref,
    owner_ref,
    gate_ref,
    latents_ref,
    wl_hbm,
    text_ref,
    cot_ref,
    wo_ref,
    wq_hbm,
    gain_ref,
    bias_ref,
    pos_ref,
    out_ref,
    grad_ref,
    wl_ref,
    wq_ref,
    lat,
    pairs_ref,
    kv_ref,
    text_all,
    cot_all,
    wo_all,
    picked,
    far_picked,
    stored,
    ctx_ref,
    product,
    own,
    gsend,
    grecv,
    hsend,
    hrecv,
    same,
    other,
    lsem,
    zsend,
    zrecv,
    xsend,
    xrecv,
    fsend,
    frecv,
    tsend,
    trecv,
    tpsend,
    tprecv,
    csend,
    crecv,
    cpsend,
    cprecv,
    wsend,
    wrecv,
    wxs,
    wxr,
    xs,
    xr,
    zs,
    zr,
    ys,
    yr,
    ps,
    pr,
    *slots,
):
    z, x, y, c = position()
    me = 2 * y + c
    ups = ({"z": lax.rem(z + 1, NZ)}, {"z": lax.rem(z + NZ - 1, NZ)})

    def chunk_rows(ch):
        return pl.ds(ch * CHUNK_ROWS, CHUNK_ROWS)

    loads = [
        pltpu.make_async_copy(latents_ref.at[chunk_rows(ch)], lat.at[chunk_rows(ch)], lsem.at[ch])
        for ch in range(CHUNKS)
    ]
    weight_load = pltpu.make_async_copy(wl_hbm, wl_ref, lsem.at[CHUNKS])
    query_load = pltpu.make_async_copy(wq_hbm, wq_ref, lsem.at[CHUNKS + 1])
    weight_load.start()
    loads[0].start()
    wait_peers = meet([*ups, *x_peers(x), *fsdp_peers(y, c)])
    started = []

    def go(copy):
        copy.start()
        started.append(copy)
        return copy

    held = ([pairs_ref, *slots[: HALF_Z - 1]], [pairs_ref, *slots[HALF_Z - 1 :]])

    def zcopy(direction, k, ch):
        images = pl.ds(ch * CHUNK_IMG, CHUNK_IMG)
        return remote(
            held[direction][k - 1].at[images],
            held[direction][k].at[images],
            zsend.at[direction, k, ch],
            zrecv.at[direction, k, ch],
            ups[direction],
        )

    def find(place, plane, dx):
        first = 3 * (NX * plane + lax.rem(x + dx, NX))
        for s in range(3):
            for k in range(5):
                ref = refs_ref[k, first + s]
                row = owner_ref[jnp.maximum(ref, 0)]
                stored[place * 15 + s * 5 + k] = jnp.where(ref >= 0, row, -1000)

    def within(place, plane):
        base = IMG * (NX * plane + x)
        wanted = 0
        for e in range(15):
            at = stored[place * 15 + e] - base
            wanted = wanted + jnp.where((at >= 0) & (at < IMG), at, 0)
        return wanted

    zcopies = {}

    def hop(direction, k, ch):
        zcopies[direction, k, ch] = go(zcopy(direction, k, ch))

    text_ring = YRing(text_ref, text_all, y, c, tsend, trecv, tpsend, tprecv)
    cot_ring = YRing(cot_ref, cot_all, y, c, csend, crecv, cpsend, cprecv)

    for dx in range(NX):
        find(dx, z, dx)
    weight_load.wait()
    for load in loads[1:]:
        load.start()
    for ch in range(CHUNKS):
        loads[ch].wait()
        pairs_ref[ch * CHUNK_IMG : (ch + 1) * CHUNK_IMG] = (
            jnp.dot(lat[chunk_rows(ch), :], wl_ref[...], preferred_element_type=F32)
            .astype(BF16)
            .reshape(CHUNK_IMG, LAT, 256)
        )
        if ch == 0:
            wait_peers()
            text_ring.begin()
        for d in range(2):
            hop(d, 1, ch)

    xcopies = []

    def deliver(block, kk):
        for dx in (1, 2, 3, 0):
            image = block[within(dx, lax.rem(z + NZ - kk, NZ))]
            if dx == 0:
                kv_ref[kk] = image
            else:
                picked[dx - 1, kk] = image
                xcopies.append(
                    go(
                        remote(
                            picked.at[dx - 1, kk],
                            kv_ref.at[dx * NZ + kk],
                            xsend.at[dx - 1, kk],
                            xrecv.at[dx - 1, kk],
                            {"x": lax.rem(x + dx, NX)},
                        )
                    )
                )

    far_up, far_down = lax.rem(z + NZ - HALF_Z + 1, NZ), lax.rem(z + HALF_Z - 1, NZ)
    far = [(1, 0, far_up), (2, 0, far_up), (3, 1, far_down), (0, 1, far_down)]
    far_copies = []

    def find_far():
        for dx, direction, _ in far:
            find(NX + dx, ups[direction]["z"], dx)

    def deliver_far():
        for dx, direction, source in far:
            far_picked[dx] = held[direction][HALF_Z - 1][within(NX + dx, source)]
            where = {"z": ups[direction]["z"], "x": lax.rem(x + dx, NX)}
            far_copies.append(
                go(
                    remote(
                        far_picked.at[dx],
                        kv_ref.at[dx * NZ + HALF_Z],
                        fsend.at[dx],
                        frecv.at[dx],
                        where if dx else ups[direction],
                    )
                )
            )

    def fsdp_place(index, sign):
        if index == 0:
            return y, 1 - c
        step = (index + 1) // 2
        row = lax.rem(y + (step if sign > 0 else NY - step), NY)
        return row, lax.rem(c + (index + 1) % 2, 2)

    quarter = pl.ds(pl.multiple_of(x * QUARTER, QUARTER), QUARTER)

    def weight_columns(row, core):
        return pl.ds(pl.multiple_of((2 * row + core) * 256, 256), 256)

    own_weight = pltpu.make_async_copy(
        wo_ref.at[quarter, weight_columns(y, c)], wo_all.at[me, quarter], lsem.at[CHUNKS + 2]
    )

    def send_weight(index):
        row, core = fsdp_place(index, 1)
        go(
            remote(
                wo_ref.at[quarter, weight_columns(row, core)],
                wo_all.at[me, quarter],
                wsend.at[index],
                wrecv.at[index],
                {"y": row, "c": core},
            )
        )

    def spread_weight():
        own_weight.wait()
        for index in range(GROUP - 1):
            row, core = fsdp_place(index, -1)
            there = wo_all.at[2 * row + core, quarter]
            remote(there, there, wsend.at[index], wrecv.at[index], {"y": row, "c": core}).wait_recv()
        for dx in range(1, NX):
            mine = wo_all.at[:, quarter]
            go(remote(mine, mine, wxs.at[dx], wxr.at[dx], {"x": lax.rem(x + dx, NX)}))

    def weight_spread():
        for dx in range(1, NX):
            rows = pl.ds(pl.multiple_of(lax.rem(x + NX - dx, NX) * QUARTER, QUARTER), QUARTER)
            there = wo_all.at[:, rows]
            remote(there, there, wxs.at[dx], wxr.at[dx], {"x": lax.rem(x + dx, NX)}).wait_recv()

    state = {}
    width = GROUP * 256

    def norm_mean():
        text_ring.finish()
        total = jnp.zeros((TOK, 128), F32)
        for f in range(GROUP):
            block = text_all[f].astype(F32)
            total = total + block[:, :128] + block[:, 128:]
        state["mean"] = jnp.sum(total, axis=-1, keepdims=True) / width

    def norm_scale():
        total = jnp.zeros((TOK, 128), F32)
        for f in range(GROUP):
            centered = text_all[f].astype(F32) - state["mean"]
            squared = centered * centered
            total = total + squared[:, :128] + squared[:, 128:]
        state["scale"] = lax.rsqrt(jnp.sum(total, axis=-1, keepdims=True) / width + EPSILON)

    def project(first, last):
        acc = state.get("acc", jnp.zeros((TOK, 128), F32))
        for f in range(first, last):
            centered = text_all[f].astype(F32) - state["mean"]
            normed = (centered * state["scale"] * gain_ref[:, f * 256 : (f + 1) * 256] + bias_ref[:, f * 256 : (f + 1) * 256]).astype(BF16)
            acc = acc + jnp.dot(normed, wq_ref[f * 256 : (f + 1) * 256, :], preferred_element_type=F32)
        state["acc"] = acc

    todo = {}

    def at_turn(turn, action, *args):
        todo.setdefault(turn, []).append(functools.partial(action, *args))

    for k in range(1, HALF_Y + 1):
        at_turn(2 * k, text_ring.step, k)
        at_turn(2 * k + 10, cot_ring.step, k)
    at_turn(2, own_weight.start)
    at_turn(3, query_load.start)
    for at, index in enumerate([7, 8, 9, 5, 6, 10, 3, 4, 11, 12, 1, 2, 13, 14, 0]):
        at_turn(4 + at // 4, send_weight, index)
    at_turn(7, cot_ring.begin)
    at_turn(9, query_load.wait)
    at_turn(11, norm_mean)
    at_turn(13, norm_scale)
    at_turn(15, project, 0, 8)
    at_turn(17, project, 8, 16)
    at_turn(13, spread_weight)

    at_turn(16, find_far)
    deliver(pairs_ref, 0)
    turn = 0
    for k in range(1, HALF_Z):
        for ch in range(CHUNKS):
            for d in range(2):
                zcopies[d, k, ch].wait_recv()
                if k < HALF_Z - 1:
                    hop(d, k + 1, ch)
            for action in todo.get(turn, ()):
                action()
            turn += 1
        if k == HALF_Z - 1:
            deliver_far()
        deliver(held[0][k], k)
        deliver(held[1][k], NZ - k)

    queries = (state["acc"] * 128 ** (-0.5)).astype(BF16)
    cot_ring.finish()
    for copy in [*xcopies, *far_copies]:
        copy.wait_recv()

    def arrival(entry):
        owner = lax.div(jnp.maximum(stored[entry], 0), IMG)
        from_x = lax.rem(x + NX - lax.rem(owner, NX), NX)
        return from_x * NZ + lax.rem(z + NZ - lax.div(owner, NX), NZ)

    square = (LAT, LAT)
    diagonal = lax.broadcasted_iota(jnp.int32, square, 0) == lax.broadcasted_iota(jnp.int32, square, 1)
    column = (lax.broadcasted_iota(jnp.int32, (LAT, 5 * LAT), 1) // LAT).astype(F32)
    for s in range(3):
        rows = slice(s * LAT, (s + 1) * LAT)
        blocks = [kv_ref[arrival(s * 5 + k)] for k in range(5)]
        keys = jnp.concatenate([b[:, :128] for b in blocks], axis=0)
        values = jnp.concatenate([b[:, 128:] for b in blocks], axis=0)
        scores = lax.dot_general(queries[rows], keys, (((1,), (1,)), ((), ())), preferred_element_type=F32)
        pos = jnp.sum(jnp.where(diagonal, pos_ref[s : s + 1, :].astype(F32), 0.0), axis=1, keepdims=True)
        scores = jnp.where(pos == column, scores, -1e30)
        weights = jnp.exp(scores - jnp.max(scores, axis=-1, keepdims=True))
        probs = (weights / jnp.sum(weights, axis=-1, keepdims=True)).astype(BF16)
        mixed = jnp.dot(probs, values, preferred_element_type=F32)
        ctx_ref[rows, :] = jnp.where(pos >= 0, mixed, 0.0).astype(BF16)

    zpeers = [{"z": lax.rem(z + kk, NZ)} for kk in range(NZ)]
    xpeers = x_peers(x)
    partner = {"c": 1 - c}
    context = ctx_ref[...]
    gcopies = {}
    ycopies = {}
    pcopies = {}
    first = True
    for kk in FAR_FIRST:
        block = cot_all[lax.rem(z + kk, NZ)]
        product[kk] = lax.dot_general(block, context, (((0,), (0,)), ((), ())), preferred_element_type=F32)
        for dx in (1, 2, 3, 0):
            part = product[kk, pl.ds(pl.multiple_of(lax.rem(x + dx, NX) * 64, 64), 64), :]
            if dx == 0:
                own[kk] = part
            else:
                gsend[dx - 1, kk] = part.astype(BF16)
                gcopies[dx, kk] = go(
                    remote(
                        gsend.at[dx - 1, kk],
                        grecv.at[dx - 1, kk],
                        xs.at[dx - 1, kk],
                        xr.at[dx - 1, kk],
                        xpeers[dx - 1],
                    )
                )
        if first:
            first = False
            for dy in (4, 3, 5, 2, 6, 1, 7):
                ycopies[dy] = go(
                    remote(ctx_ref, same.at[dy], ys.at[dy], yr.at[dy], {"y": lax.rem(y + dy, NY)})
                )
            pcopies[0] = go(remote(ctx_ref, other.at[0], ps.at[0], pr.at[0], partner))

    def pass_on(dy):
        ycopies[dy].wait_recv()
        pcopies[dy] = go(remote(same.at[dy], other.at[dy], ps.at[dy], pr.at[dy], partner))

    passing = {9: (4, 3, 5), 11: (2, 6), 13: (1, 7)}
    hcopies = {}
    for at, kk in enumerate(FAR_FIRST):
        total = own[kk]
        for dx in range(1, NX):
            gcopies[dx, kk].wait_recv()
            total = total + grecv[dx - 1, kk].astype(F32)
        if kk == 0:
            own[0] = total
        else:
            hsend[kk] = total.astype(BF16)
            hcopies[kk] = go(remote(hsend.at[kk], hrecv.at[kk], zs.at[kk], zr.at[kk], zpeers[kk]))
        for dy in passing.get(at, ()):
            pass_on(dy)
    weight_spread()
    gate = gate_ref[0]
    update = jnp.dot(context, wo_all[me], preferred_element_type=F32)
    for dy in range(1, NY):
        row = 2 * lax.rem(y + NY - dy, NY)
        update = update + jnp.dot(same[dy], wo_all[row + c], preferred_element_type=F32)
    for dy in (0, 4, 3, 5, 2, 6, 1, 7):
        row = 2 * lax.rem(y + NY - dy, NY)
        pcopies[dy].wait_recv()
        update = update + jnp.dot(other[dy], wo_all[row + 1 - c], preferred_element_type=F32)
    out_ref[...] = (text_all[me].astype(F32) + gate * update).astype(BF16)
    total = own[0]
    for kk in FAR_FIRST[::-1][1:]:
        hcopies[kk].wait_recv()
        total = total + hrecv[kk].astype(F32)
    grad_ref[...] = gate * total
    for copy in started:
        copy.wait_send()


def fused_call(refs, owner, gate, latents, wl, text, cot, wo, wq, gain, bias, pos):
    vmem = pl.BlockSpec(memory_space=pltpu.VMEM)
    smem = pl.BlockSpec(memory_space=pltpu.SMEM)
    dma = pltpu.SemaphoreType.DMA
    ring = [dma((2, HALF_Y + 1)), dma((2, HALF_Y + 1)), dma((NY + 1,)), dma((NY,))]
    return pl.pallas_call(
        fused_kernel,
        out_shape=(jax.ShapeDtypeStruct((TOK, 256), BF16), jax.ShapeDtypeStruct((64, 128), F32)),
        in_specs=[smem] * 3 + [pl.BlockSpec(memory_space=pltpu.HBM)] * 6 + [vmem] * 3,
        out_specs=(vmem, vmem),
        scratch_shapes=[
            pltpu.VMEM((GROUP * 256, 256), BF16),
            pltpu.VMEM((GROUP * 256, 128), BF16),
            pltpu.VMEM((IMG * LAT, GROUP * 256), BF16),
            pltpu.VMEM((IMG, LAT, 256), BF16),
            pltpu.VMEM((NX * NZ, LAT, 256), BF16),
            pltpu.VMEM((GROUP, TOK, 256), BF16),
            pltpu.VMEM((GROUP, TOK, 256), BF16),
            pltpu.VMEM((GROUP, 128, 256), BF16),
            pltpu.VMEM((NX - 1, NZ, LAT, 256), BF16),
            pltpu.VMEM((NX, LAT, 256), BF16),
            pltpu.SMEM((2 * NX * 15,), jnp.int32),
            pltpu.VMEM((TOK, 128), BF16),
            pltpu.VMEM((NZ, 256, 128), F32),
            pltpu.VMEM((NZ, 64, 128), F32),
            pltpu.VMEM((NX - 1, NZ, 64, 128), BF16),
            pltpu.VMEM((NX - 1, NZ, 64, 128), BF16),
            pltpu.VMEM((NZ, 64, 128), BF16),
            pltpu.VMEM((NZ, 64, 128), BF16),
            pltpu.VMEM((NY, TOK, 128), BF16),
            pltpu.VMEM((NY, TOK, 128), BF16),
            dma((CHUNKS + 3,)),
            dma((2, HALF_Z, CHUNKS)),
            dma((2, HALF_Z, CHUNKS)),
            dma((NX - 1, NZ)),
            dma((NX - 1, NZ)),
            dma((NX,)),
            dma((NX,)),
            *ring,
            *ring,
            dma((GROUP - 1,)),
            dma((GROUP - 1,)),
            dma((NX,)),
            dma((NX,)),
            dma((NX - 1, NZ)),
            dma((NX - 1, NZ)),
            dma((NZ,)),
            dma((NZ,)),
            dma((NY,)),
            dma((NY,)),
            dma((NY,)),
            dma((NY,)),
        ]
        + [pltpu.VMEM((IMG, LAT, 256), BF16)] * (2 * (HALF_Z - 1)),
        compiler_params=pltpu.CompilerParams(
            collective_id=0, has_side_effects=True, vmem_limit_bytes=62 << 20
        ),
        name="fused",
    )(refs, owner, gate, latents, wl, text, cot, wo, wq, gain, bias, pos)


def body(
    text_states,
    cotangent,
    norm_gain,
    norm_bias,
    branch_gate,
    query_weight,
    latent_weight,
    output_weight,
    latents,
    media_refs,
    media_pos,
    owner_map,
):
    layer_out, out_grad = fused_call(
        media_refs.T,
        owner_map,
        jnp.tanh(branch_gate),
        latents.reshape(IMG * LAT, -1),
        latent_weight.reshape(-1, 256),
        text_states.reshape(TOK, 256),
        cotangent.reshape(TOK, 256),
        output_weight.reshape(128, -1),
        query_weight.reshape(-1, 128),
        norm_gain.reshape(1, -1),
        norm_bias.reshape(1, -1),
        media_pos,
    )
    return layer_out.reshape(3, 64, 256), jnp.transpose(out_grad, (1, 0))[None]


def solution(mesh):
    split = Mesh(mesh.devices.reshape(NZ, NX, NY, 2), ("z", "x", "y", "c"))
    dp, fsdp = ("z", "x"), ("y", "c")
    return jax.shard_map(
        body,
        mesh=split,
        in_specs=(
            P(dp, None, fsdp),
            P(dp, None, fsdp),
            P(),
            P(),
            P(),
            P(None, fsdp, None),
            P(None, fsdp, None),
            P(fsdp, None, None),
            P(dp, None, None),
            P(),
            P(dp, None),
            P(),
        ),
        out_specs=(P(dp, None, fsdp), P(fsdp, None, dp)),
        check_vma=False,
    )
```

```python
import functools

import jax
import jax.numpy as jnp
from jax import lax
from jax.experimental import pallas as pl
from jax.experimental.pallas import tpu as pltpu
from jax.sharding import Mesh
from jax.sharding import PartitionSpec as P

EPSILON = 1e-05
MESH = pl.DeviceIdType.MESH
NZ, NX, NY = 16, 4, 8
GROUP = 2 * NY
IMG = 9
LAT = 64
TOK = 192
CHUNKS = 3
CHUNK_IMG = IMG // CHUNKS
CHUNK_ROWS = CHUNK_IMG * LAT
QUARTER = 128 // NX
BEHIND = 6
HALF_Z = NZ // 2
HALF_Y = NY // 2
BF16 = jnp.bfloat16
F32 = jnp.float32


def remote(src, dst, send, recv, where):
    return pltpu.make_async_remote_copy(
        src_ref=src, dst_ref=dst, send_sem=send, recv_sem=recv, device_id=where, device_id_type=MESH
    )


def position():
    return lax.axis_index("z"), lax.axis_index("x"), lax.axis_index("y"), lax.axis_index("c")


def meet(targets):
    barrier = pltpu.get_barrier_semaphore()
    for where in targets:
        pl.semaphore_signal(barrier, inc=1, device_id=where, device_id_type=MESH)
    return lambda: pl.semaphore_wait(barrier, len(targets))


def fsdp_peers(y, c):
    peers = [{"c": 1 - c}]
    for dy in range(1, NY):
        for dc in range(2):
            peers.append({"y": lax.rem(y + dy, NY), "c": lax.rem(c + dc, 2)})
    return peers


def x_peers(x):
    return [{"x": lax.rem(x + dx, NX)} for dx in range(1, NX)]


class YRing:
    def __init__(self, own, full, y, c, send, recv, psend, precv):
        self.own, self.full, self.y, self.c = own, full, y, c
        self.send, self.recv, self.psend, self.precv = send, recv, psend, precv
        self.started = []

    def slot(self, direction, k, core):
        row = lax.rem(self.y + (NY - k if direction == 0 else k), NY)
        return self.full.at[2 * row + core]

    def neighbour(self, direction):
        return {"y": lax.rem(self.y + (1 if direction == 0 else NY - 1), NY)}

    def hop(self, direction, k):
        src = self.own if k == 1 else self.slot(direction, k - 1, self.c)
        dst = self.slot(direction, k - 1, self.c)
        copy = remote(src, dst, self.send.at[direction, k], self.recv.at[direction, k], self.neighbour(direction))
        copy.start()
        self.started.append(copy)

    def to_partner(self, src, dst, index):
        copy = remote(src, dst, self.psend.at[index], self.precv.at[index], {"c": 1 - self.c})
        copy.start()
        self.started.append(copy)

    def begin(self):
        self.hop(0, 1)
        self.hop(1, 1)
        mine = self.slot(0, 0, self.c)
        self.to_partner(self.own, mine, 0)
        self.local = pltpu.make_async_copy(self.own, mine, self.psend.at[NY])
        self.local.start()

    def step(self, k):
        for direction, last in ((0, HALF_Y), (1, HALF_Y - 1)):
            if k <= last:
                here = self.slot(direction, k, self.c)
                remote(
                    here, here, self.send.at[direction, k], self.recv.at[direction, k], self.neighbour(direction)
                ).wait_recv()
                if k < last:
                    self.hop(direction, k + 1)
                self.to_partner(here, here, k + (HALF_Y if direction else 0))

    def finish(self):
        self.local.wait()
        for direction, last in ((0, HALF_Y), (1, HALF_Y - 1)):
            for k in range(0 if direction == 0 else 1, last + 1):
                index = k + (HALF_Y if direction else 0)
                there = self.slot(direction, k, 1 - self.c)
                remote(
                    there, there, self.psend.at[index], self.precv.at[index], {"c": 1 - self.c}
                ).wait_recv()
        for copy in self.started:
            copy.wait_send()


FAR_FIRST = [8, 7, 9, 6, 10, 5, 11, 4, 12, 3, 13, 2, 14, 1, 15, 0]


def fused_kernel(
    refs_ref,
    owner_ref,
    gate_ref,
    latents_ref,
    wl_hbm,
    text_ref,
    cot_ref,
    wo_ref,
    wq_hbm,
    gain_ref,
    bias_ref,
    pos_ref,
    out_ref,
    grad_ref,
    wl_ref,
    wq_ref,
    lat,
    pairs_ref,
    kv_ref,
    text_all,
    cot_all,
    wo_all,
    picked,
    far_picked,
    stored,
    ctx_ref,
    product,
    own,
    gsend,
    grecv,
    hsend,
    hrecv,
    same,
    other,
    lsem,
    zsend,
    zrecv,
    xsend,
    xrecv,
    fsend,
    frecv,
    tsend,
    trecv,
    tpsend,
    tprecv,
    csend,
    crecv,
    cpsend,
    cprecv,
    wsend,
    wrecv,
    wxs,
    wxr,
    xs,
    xr,
    zs,
    zr,
    ys,
    yr,
    ps,
    pr,
    *slots,
):
    z, x, y, c = position()
    me = 2 * y + c
    ups = ({"z": lax.rem(z + 1, NZ)}, {"z": lax.rem(z + NZ - 1, NZ)})

    def chunk_rows(ch):
        return pl.ds(ch * CHUNK_ROWS, CHUNK_ROWS)

    loads = [
        pltpu.make_async_copy(latents_ref.at[chunk_rows(ch)], lat.at[chunk_rows(ch)], lsem.at[ch])
        for ch in range(CHUNKS)
    ]
    weight_load = pltpu.make_async_copy(wl_hbm, wl_ref, lsem.at[CHUNKS])
    query_load = pltpu.make_async_copy(wq_hbm, wq_ref, lsem.at[CHUNKS + 1])
    weight_load.start()
    loads[0].start()
    wait_peers = meet([*ups, *x_peers(x), *fsdp_peers(y, c)])
    started = []

    def go(copy):
        copy.start()
        started.append(copy)
        return copy

    held = ([pairs_ref, *slots[: HALF_Z - 1]], [pairs_ref, *slots[HALF_Z - 1 :]])

    def zcopy(direction, k, ch):
        images = pl.ds(ch * CHUNK_IMG, CHUNK_IMG)
        return remote(
            held[direction][k - 1].at[images],
            held[direction][k].at[images],
            zsend.at[direction, k, ch],
            zrecv.at[direction, k, ch],
            ups[direction],
        )

    def find(place, plane, dx):
        first = 3 * (NX * plane + lax.rem(x + dx, NX))
        for s in range(3):
            for k in range(5):
                ref = refs_ref[k, first + s]
                row = owner_ref[jnp.maximum(ref, 0)]
                stored[place * 15 + s * 5 + k] = jnp.where(ref >= 0, row, -1000)

    def within(place, plane):
        base = IMG * (NX * plane + x)
        wanted = 0
        for e in range(15):
            at = stored[place * 15 + e] - base
            wanted = wanted + jnp.where((at >= 0) & (at < IMG), at, 0)
        return wanted

    zcopies = {}

    def hop(direction, k, ch):
        zcopies[direction, k, ch] = go(zcopy(direction, k, ch))

    text_ring = YRing(text_ref, text_all, y, c, tsend, trecv, tpsend, tprecv)
    cot_ring = YRing(cot_ref, cot_all, y, c, csend, crecv, cpsend, cprecv)

    for dx in range(NX):
        find(dx, z, dx)
    weight_load.wait()
    for load in loads[1:]:
        load.start()
    for ch in range(CHUNKS):
        loads[ch].wait()
        pairs_ref[ch * CHUNK_IMG : (ch + 1) * CHUNK_IMG] = (
            jnp.dot(lat[chunk_rows(ch), :], wl_ref[...], preferred_element_type=F32)
            .astype(BF16)
            .reshape(CHUNK_IMG, LAT, 256)
        )
        if ch == 0:
            wait_peers()
            text_ring.begin()
        for d in range(2):
            hop(d, 1, ch)

    xcopies = []

    choices = {}

    def choose(kk):
        choices[kk] = [within(dx, lax.rem(z + NZ - kk, NZ)) for dx in range(NX)]

    def deliver(block, kk):
        for dx in (1, 2, 3, 0):
            image = block[choices[kk][dx]]
            if dx == 0:
                kv_ref[kk] = image
            else:
                picked[dx - 1, kk] = image
                xcopies.append(
                    go(
                        remote(
                            picked.at[dx - 1, kk],
                            kv_ref.at[dx * NZ + kk],
                            xsend.at[dx - 1, kk],
                            xrecv.at[dx - 1, kk],
                            {"x": lax.rem(x + dx, NX)},
                        )
                    )
                )

    far_up, far_down = lax.rem(z + NZ - HALF_Z + 1, NZ), lax.rem(z + HALF_Z - 1, NZ)
    far = [(1, 0, far_up), (2, 0, far_up), (3, 1, far_down), (0, 1, far_down)]
    far_copies = []

    def find_far():
        for dx, direction, _ in far:
            find(NX + dx, ups[direction]["z"], dx)

    def choose_far():
        choices["far"] = {dx: within(NX + dx, source) for dx, _, source in far}

    def deliver_far():
        for dx, direction, _ in far:
            far_picked[dx] = held[direction][HALF_Z - 1][choices["far"][dx]]
            where = {"z": ups[direction]["z"], "x": lax.rem(x + dx, NX)}
            far_copies.append(
                go(
                    remote(
                        far_picked.at[dx],
                        kv_ref.at[dx * NZ + HALF_Z],
                        fsend.at[dx],
                        frecv.at[dx],
                        where if dx else ups[direction],
                    )
                )
            )

    def fsdp_place(index, sign):
        if index == 0:
            return y, 1 - c
        step = (index + 1) // 2
        row = lax.rem(y + (step if sign > 0 else NY - step), NY)
        return row, lax.rem(c + (index + 1) % 2, 2)

    quarter = pl.ds(pl.multiple_of(x * QUARTER, QUARTER), QUARTER)

    def weight_columns(row, core):
        return pl.ds(pl.multiple_of((2 * row + core) * 256, 256), 256)

    own_weight = pltpu.make_async_copy(
        wo_ref.at[quarter, weight_columns(y, c)], wo_all.at[me, quarter], lsem.at[CHUNKS + 2]
    )

    def send_weight(index):
        row, core = fsdp_place(index, 1)
        go(
            remote(
                wo_ref.at[quarter, weight_columns(row, core)],
                wo_all.at[me, quarter],
                wsend.at[index],
                wrecv.at[index],
                {"y": row, "c": core},
            )
        )

    def spread_weight():
        own_weight.wait()
        for index in range(GROUP - 1):
            row, core = fsdp_place(index, -1)
            there = wo_all.at[2 * row + core, quarter]
            remote(there, there, wsend.at[index], wrecv.at[index], {"y": row, "c": core}).wait_recv()
        for dx in range(1, NX):
            mine = wo_all.at[:, quarter]
            go(remote(mine, mine, wxs.at[dx], wxr.at[dx], {"x": lax.rem(x + dx, NX)}))

    def weight_spread():
        for dx in range(1, NX):
            rows = pl.ds(pl.multiple_of(lax.rem(x + NX - dx, NX) * QUARTER, QUARTER), QUARTER)
            there = wo_all.at[:, rows]
            remote(there, there, wxs.at[dx], wxr.at[dx], {"x": lax.rem(x + dx, NX)}).wait_recv()

    state = {}
    width = GROUP * 256

    def norm_mean():
        text_ring.finish()
        total = jnp.zeros((TOK, 128), F32)
        for f in range(GROUP):
            block = text_all[f].astype(F32)
            total = total + block[:, :128] + block[:, 128:]
        state["mean"] = jnp.sum(total, axis=-1, keepdims=True) / width

    def norm_scale():
        total = jnp.zeros((TOK, 128), F32)
        for f in range(GROUP):
            centered = text_all[f].astype(F32) - state["mean"]
            squared = centered * centered
            total = total + squared[:, :128] + squared[:, 128:]
        state["scale"] = lax.rsqrt(jnp.sum(total, axis=-1, keepdims=True) / width + EPSILON)

    def project(first, last):
        acc = state.get("acc", jnp.zeros((TOK, 128), F32))
        for f in range(first, last):
            centered = text_all[f].astype(F32) - state["mean"]
            normed = (centered * state["scale"] * gain_ref[:, f * 256 : (f + 1) * 256] + bias_ref[:, f * 256 : (f + 1) * 256]).astype(BF16)
            acc = acc + jnp.dot(normed, wq_ref[f * 256 : (f + 1) * 256, :], preferred_element_type=F32)
        state["acc"] = acc

    todo = {}

    def at_turn(turn, action, *args):
        todo.setdefault(turn, []).append(functools.partial(action, *args))

    for k in range(1, HALF_Y + 1):
        at_turn(2 * k, text_ring.step, k)
        at_turn(2 * k + 10, cot_ring.step, k)
    at_turn(2, own_weight.start)
    at_turn(3, query_load.start)
    for at, index in enumerate([7, 8, 9, 5, 6, 10, 3, 4, 11, 12, 1, 2, 13, 14, 0]):
        at_turn(4 + at // 4, send_weight, index)
    at_turn(7, cot_ring.begin)
    at_turn(9, query_load.wait)
    at_turn(11, norm_mean)
    at_turn(13, norm_scale)
    at_turn(15, project, 0, 8)
    at_turn(17, project, 8, 16)
    at_turn(13, spread_weight)

    def arrival(entry):
        owner = lax.div(jnp.maximum(stored[entry], 0), IMG)
        from_x = lax.rem(x + NX - lax.rem(owner, NX), NX)
        return from_x * NZ + lax.rem(z + NZ - lax.div(owner, NX), NZ)

    arrivals = []
    at_turn(19, lambda: arrivals.extend(arrival(entry) for entry in range(15)))
    at_turn(16, find_far)
    at_turn(18, choose_far)
    for k in range(1, HALF_Z):
        at_turn(3 * k - 3, choose, k)
        at_turn(3 * k - 3, choose, NZ - k)
    choose(0)
    deliver(pairs_ref, 0)
    turn = 0
    for k in range(1, HALF_Z):
        for ch in range(CHUNKS):
            for d in range(2):
                zcopies[d, k, ch].wait_recv()
                if k < HALF_Z - 1:
                    hop(d, k + 1, ch)
            for action in todo.get(turn, ()):
                action()
            turn += 1
        if k == HALF_Z - 1:
            deliver_far()
        deliver(held[0][k], k)
        deliver(held[1][k], NZ - k)

    queries = (state["acc"] * 128 ** (-0.5)).astype(BF16)
    cot_ring.finish()
    for copy in [*xcopies, *far_copies]:
        copy.wait_recv()

    square = (LAT, LAT)
    diagonal = lax.broadcasted_iota(jnp.int32, square, 0) == lax.broadcasted_iota(jnp.int32, square, 1)
    column = (lax.broadcasted_iota(jnp.int32, (LAT, 5 * LAT), 1) // LAT).astype(F32)
    for s in range(3):
        rows = slice(s * LAT, (s + 1) * LAT)
        blocks = [kv_ref[arrivals[s * 5 + k]] for k in range(5)]
        keys = jnp.concatenate([b[:, :128] for b in blocks], axis=0)
        values = jnp.concatenate([b[:, 128:] for b in blocks], axis=0)
        scores = lax.dot_general(queries[rows], keys, (((1,), (1,)), ((), ())), preferred_element_type=F32)
        pos = jnp.sum(jnp.where(diagonal, pos_ref[s : s + 1, :].astype(F32), 0.0), axis=1, keepdims=True)
        scores = jnp.where(pos == column, scores, -1e30)
        weights = jnp.exp(scores - jnp.max(scores, axis=-1, keepdims=True))
        probs = (weights / jnp.sum(weights, axis=-1, keepdims=True)).astype(BF16)
        mixed = jnp.dot(probs, values, preferred_element_type=F32)
        ctx_ref[rows, :] = jnp.where(pos >= 0, mixed, 0.0).astype(BF16)

    zpeers = [{"z": lax.rem(z + kk, NZ)} for kk in range(NZ)]
    xpeers = x_peers(x)
    partner = {"c": 1 - c}
    context = ctx_ref[...]
    gcopies = {}
    ycopies = {}
    pcopies = {}

    def send_parts(kk):
        block = cot_all[lax.rem(z + kk, NZ)]
        product[kk] = lax.dot_general(block, context, (((0,), (0,)), ((), ())), preferred_element_type=F32)
        for dx in (1, 2, 3, 0):
            part = product[kk, pl.ds(pl.multiple_of(lax.rem(x + dx, NX) * 64, 64), 64), :]
            if dx == 0:
                own[kk] = part
            else:
                gsend[dx - 1, kk] = part.astype(BF16)
                gcopies[dx, kk] = go(
                    remote(
                        gsend.at[dx - 1, kk],
                        grecv.at[dx - 1, kk],
                        xs.at[dx - 1, kk],
                        xr.at[dx - 1, kk],
                        xpeers[dx - 1],
                    )
                )

    def send_context():
        for dy in (4, 3, 5, 2, 6, 1, 7):
            ycopies[dy] = go(
                remote(ctx_ref, same.at[dy], ys.at[dy], yr.at[dy], {"y": lax.rem(y + dy, NY)})
            )
        pcopies[0] = go(remote(ctx_ref, other.at[0], ps.at[0], pr.at[0], partner))

    def pass_on(dy):
        ycopies[dy].wait_recv()
        pcopies[dy] = go(remote(same.at[dy], other.at[dy], ps.at[dy], pr.at[dy], partner))

    hcopies = {}

    def send_sum(kk):
        total = own[kk]
        for dx in range(1, NX):
            gcopies[dx, kk].wait_recv()
            total = total + grecv[dx - 1, kk].astype(F32)
        if kk == 0:
            own[0] = total
        else:
            hsend[kk] = total.astype(BF16)
            hcopies[kk] = go(remote(hsend.at[kk], hrecv.at[kk], zs.at[kk], zr.at[kk], zpeers[kk]))

    passing = {9: (4, 3, 5), 11: (2, 6), 13: (1, 7)}
    for at in range(NZ + BEHIND):
        if at < NZ:
            send_parts(FAR_FIRST[at])
        if at == 0:
            send_context()
        if at >= BEHIND:
            send_sum(FAR_FIRST[at - BEHIND])
            for dy in passing.get(at - BEHIND, ()):
                pass_on(dy)
    weight_spread()
    gate = gate_ref[0]
    update = jnp.dot(context, wo_all[me], preferred_element_type=F32)
    for dy in range(1, NY):
        row = 2 * lax.rem(y + NY - dy, NY)
        update = update + jnp.dot(same[dy], wo_all[row + c], preferred_element_type=F32)
    for dy in (0, 4, 3, 5, 2, 6, 1, 7):
        row = 2 * lax.rem(y + NY - dy, NY)
        pcopies[dy].wait_recv()
        update = update + jnp.dot(other[dy], wo_all[row + 1 - c], preferred_element_type=F32)
    out_ref[...] = (text_all[me].astype(F32) + gate * update).astype(BF16)
    total = own[0]
    for kk in FAR_FIRST[::-1][1:]:
        hcopies[kk].wait_recv()
        total = total + hrecv[kk].astype(F32)
    grad_ref[...] = gate * total
    for copy in started:
        copy.wait_send()


def fused_call(refs, owner, gate, latents, wl, text, cot, wo, wq, gain, bias, pos):
    vmem = pl.BlockSpec(memory_space=pltpu.VMEM)
    smem = pl.BlockSpec(memory_space=pltpu.SMEM)
    dma = pltpu.SemaphoreType.DMA
    ring = [dma((2, HALF_Y + 1)), dma((2, HALF_Y + 1)), dma((NY + 1,)), dma((NY,))]
    return pl.pallas_call(
        fused_kernel,
        out_shape=(jax.ShapeDtypeStruct((TOK, 256), BF16), jax.ShapeDtypeStruct((64, 128), F32)),
        in_specs=[smem] * 3 + [pl.BlockSpec(memory_space=pltpu.HBM)] * 6 + [vmem] * 3,
        out_specs=(vmem, vmem),
        scratch_shapes=[
            pltpu.VMEM((GROUP * 256, 256), BF16),
            pltpu.VMEM((GROUP * 256, 128), BF16),
            pltpu.VMEM((IMG * LAT, GROUP * 256), BF16),
            pltpu.VMEM((IMG, LAT, 256), BF16),
            pltpu.VMEM((NX * NZ, LAT, 256), BF16),
            pltpu.VMEM((GROUP, TOK, 256), BF16),
            pltpu.VMEM((GROUP, TOK, 256), BF16),
            pltpu.VMEM((GROUP, 128, 256), BF16),
            pltpu.VMEM((NX - 1, NZ, LAT, 256), BF16),
            pltpu.VMEM((NX, LAT, 256), BF16),
            pltpu.SMEM((2 * NX * 15,), jnp.int32),
            pltpu.VMEM((TOK, 128), BF16),
            pltpu.VMEM((NZ, 256, 128), F32),
            pltpu.VMEM((NZ, 64, 128), F32),
            pltpu.VMEM((NX - 1, NZ, 64, 128), BF16),
            pltpu.VMEM((NX - 1, NZ, 64, 128), BF16),
            pltpu.VMEM((NZ, 64, 128), BF16),
            pltpu.VMEM((NZ, 64, 128), BF16),
            pltpu.VMEM((NY, TOK, 128), BF16),
            pltpu.VMEM((NY, TOK, 128), BF16),
            dma((CHUNKS + 3,)),
            dma((2, HALF_Z, CHUNKS)),
            dma((2, HALF_Z, CHUNKS)),
            dma((NX - 1, NZ)),
            dma((NX - 1, NZ)),
            dma((NX,)),
            dma((NX,)),
            *ring,
            *ring,
            dma((GROUP - 1,)),
            dma((GROUP - 1,)),
            dma((NX,)),
            dma((NX,)),
            dma((NX - 1, NZ)),
            dma((NX - 1, NZ)),
            dma((NZ,)),
            dma((NZ,)),
            dma((NY,)),
            dma((NY,)),
            dma((NY,)),
            dma((NY,)),
        ]
        + [pltpu.VMEM((IMG, LAT, 256), BF16)] * (2 * (HALF_Z - 1)),
        compiler_params=pltpu.CompilerParams(
            collective_id=0, has_side_effects=True, vmem_limit_bytes=62 << 20
        ),
        name="fused",
    )(refs, owner, gate, latents, wl, text, cot, wo, wq, gain, bias, pos)


def body(
    text_states,
    cotangent,
    norm_gain,
    norm_bias,
    branch_gate,
    query_weight,
    latent_weight,
    output_weight,
    latents,
    media_refs,
    media_pos,
    owner_map,
):
    layer_out, out_grad = fused_call(
        media_refs.T,
        owner_map,
        jnp.tanh(branch_gate),
        latents.reshape(IMG * LAT, -1),
        latent_weight.reshape(-1, 256),
        text_states.reshape(TOK, 256),
        cotangent.reshape(TOK, 256),
        output_weight.reshape(128, -1),
        query_weight.reshape(-1, 128),
        norm_gain.reshape(1, -1),
        norm_bias.reshape(1, -1),
        media_pos,
    )
    return layer_out.reshape(3, 64, 256), jnp.transpose(out_grad, (1, 0))[None]


def solution(mesh):
    split = Mesh(mesh.devices.reshape(NZ, NX, NY, 2), ("z", "x", "y", "c"))
    dp, fsdp = ("z", "x"), ("y", "c")
    return jax.shard_map(
        body,
        mesh=split,
        in_specs=(
            P(dp, None, fsdp),
            P(dp, None, fsdp),
            P(),
            P(),
            P(),
            P(None, fsdp, None),
            P(None, fsdp, None),
            P(fsdp, None, None),
            P(dp, None, None),
            P(),
            P(dp, None),
            P(),
        ),
        out_specs=(P(dp, None, fsdp), P(fsdp, None, dp)),
        check_vma=False,
    )
```
